256 devices in a mesh: dp: 128 (over y, z, x), blk: 2 (over core).
Axes of the slice: x: 4, y: 4, z: 8, core: 2. Of those that a mesh axis runs over, the one named last changes fastest.
Arguments:
- vectors: float32 [131072, 96], P('dp'), may hold values from -16 to 16
- codes: int32 [131072, 8], P('dp'), may hold values from 0 to 255, as said below
- weights: bfloat16 [131072], P('dp'), may hold values from 0.25 to 4
- ridge: float32 [1], replicated, may hold values from 0.1 to 0.5
Outputs:
- codebooks: float32 [8, 256, 96], replicated
- residual: float32 [131072, 96], P('dp')
- distortion: float32 [], replicated
The draws below stay inside these ranges and needn't reach their ends.
Inputs may be any that keep to these rules, and one draw needn't show every extreme that they name: `codes`: 8 codebook indices per vector.
All inputs are finite; a program needn't handle non-finite values.
Results may differ from the reference program's by a relative error of at most 0.0003.
Values sent between devices are 32-bit elements; how exact they have to be, the bound alone decides.
No kernel may reach another device: no remote copies, remote signals or barrier semaphores. Data moves between devices by JAX's collectives and lax.ppermute only.
A program may use at most 128 MiB of HBM per device.

```python
import math
import jax
import jax.numpy as jnp
from jax import lax

D = 96
K = 256
M = 8
ITERS = 8
ROWS = 131072


def shared_codes(key):
    base = jax.random.fold_in(key, 11)
    keys = jax.random.split(base, 4)
    perms = jax.vmap(lambda single: jax.random.permutation(single, K))(jax.random.split(keys[0], M))
    perms = perms.astype(jnp.int32)
    first = jax.random.randint(keys[1], (ROWS, M), 0, K).astype(jnp.int32)
    second = jax.random.randint(keys[2], (ROWS, M), 0, K).astype(jnp.int32)
    ranks = jnp.minimum(first, second)
    tied = jax.random.randint(keys[3], (ROWS, 1), 0, 2).astype(jnp.int32)
    ranks = jnp.where(tied == 1, ranks[:, :1], ranks).astype(jnp.int32)
    return perms[jnp.arange(M)[None, :], ranks].astype(jnp.int32)


def draw_codes(key, part):
    return shared_codes(key)


def draw_vectors(key, part):
    codes = shared_codes(key)
    keys = jax.random.split(jax.random.fold_in(key, 23), 2)
    truth = 0.5 * jax.random.truncated_normal(keys[0], -3.0, 3.0, (M, K, D), jnp.float32)
    recon = jnp.zeros((ROWS, D), jnp.float32)
    for book in range(M):
        recon = recon + jnp.take(truth[book], codes[:, book], axis=0)
    position = jnp.arange(ROWS, dtype=jnp.float32) / ROWS
    level = (0.3 * (1.0 + 2.0 * position))[:, None]
    noise = jax.random.truncated_normal(keys[1], -4.0, 4.0, (ROWS, D), jnp.float32)
    return recon + level * noise


def steps_of(own_key, dims, cuts, least, high):
    factor_of = 1.0
    for dim, shards_of in cuts:
        steps = jax.random.uniform(jax.random.fold_in(jax.random.fold_in(own_key, 6), dim), (shards_of,), jnp.float32, least / len(cuts), high / len(cuts))
        factor_of = factor_of * jnp.repeat(jnp.exp(steps), dims[dim] // shards_of).reshape((-1,) + (1,) * (len(dims) - 1 - dim))
    return factor_of


def setup_inputs(seed: int = 0) -> dict:
    arg_keys = jax.random.split(jax.random.key(seed), 5)
    vectors = draw_vectors(jax.random.fold_in(arg_keys[4], 71), 0)
    codes = draw_codes(jax.random.fold_in(arg_keys[4], 71), 0)
    weights = jnp.clip(jnp.exp(math.log(4.0) - 2.7725887 * jax.random.uniform(arg_keys[2], (ROWS,), jnp.float32) ** steps_of(arg_keys[2], (ROWS,), ((0, 128),), -0.2, 0.2)), 0.25, 4.0).astype(jnp.bfloat16)
    ridge = jnp.clip(jnp.exp(jax.random.uniform(arg_keys[3], (1,), jnp.float32, math.log(0.1), math.log(0.5))), 0.1, 0.5)
    return {"vectors": vectors, "codes": codes, "weights": weights, "ridge": ridge}


HIGH = lax.Precision.HIGHEST


def reference(vectors, codes, weights, ridge):
    rows = vectors.shape[0]
    mass = weights.astype(jnp.float32)
    weighted = vectors * mass[:, None]
    count_list = []
    sum_list = []
    for book in range(M):
        count_list.append(jax.ops.segment_sum(mass, codes[:, book], num_segments=K))
        sum_list.append(jax.ops.segment_sum(weighted, codes[:, book], num_segments=K))
    counts = jnp.stack(count_list)
    right = jnp.stack(sum_list).reshape(M * K, D)
    blocks = []
    for first in range(M):
        row_blocks = []
        for second in range(M):
            if first == second:
                row_blocks.append(jnp.diag(counts[first]))
            else:
                joint = codes[:, first] * K + codes[:, second]
                row_blocks.append(jax.ops.segment_sum(mass, joint, num_segments=K * K).reshape(K, K))
        blocks.append(jnp.concatenate(row_blocks, axis=1))
    gram = jnp.concatenate(blocks, axis=0)
    total_mass = jnp.sum(counts[0])
    lam = ridge[0] * total_mass / K
    precond = (counts + lam).reshape(M * K, 1)
    solution = jnp.zeros((M * K, D), jnp.float32)
    remain = right
    scaled = remain / precond
    direction = scaled
    inner = jnp.sum(remain * scaled, axis=0)
    for step in range(ITERS):
        image = jnp.dot(gram, direction, precision=HIGH) + lam * direction
        alpha = inner / jnp.sum(direction * image, axis=0)
        solution = solution + alpha * direction
        remain = remain - alpha * image
        scaled = remain / precond
        fresh = jnp.sum(remain * scaled, axis=0)
        direction = scaled + (fresh / inner) * direction
        inner = fresh
    codebooks = solution.reshape(M, K, D)
    recon = jnp.zeros_like(vectors)
    for book in range(M):
        recon = recon + jnp.take(codebooks[book], codes[:, book], axis=0)
    residual = vectors - recon
    distortion = jnp.sum(mass[:, None] * residual * residual) / (total_mass * D)
    return codebooks, residual, distortion
```

```python
import functools

import jax
import jax.numpy as jnp
from jax import lax
from jax.experimental import pallas as pl
from jax.experimental.pallas import tpu as pltpu
from jax.sharding import Mesh
from jax.sharding import PartitionSpec as P

K = 256
M = 8
D = 96
ITERS = 8
NY, NZ, NX = 4, 8, 4
DP = ("y", "z", "x")
F32 = jnp.float32
BF16 = jnp.bfloat16
NT = (((1,), (1,)), ((), ()))
NN = (((1,), (0,)), ((), ()))


def dot(a, b, dims):
    return lax.dot_general(a, b, dims, preferred_element_type=F32)


def split3(a):
    hi = a.astype(BF16).astype(F32)
    rest = a - hi
    mid = rest.astype(BF16).astype(F32)
    return hi, mid, rest - mid


def params(**more):
    return pltpu.CompilerParams(vmem_limit_bytes=48 << 20, **more)


VMEM = pl.BlockSpec(memory_space=pltpu.VMEM)
SMEM = pl.BlockSpec(memory_space=pltpu.SMEM)
ANY = pl.BlockSpec(memory_space=pl.ANY)


def message_kernel(info, codes_ref, mass_ref, vectors_ref, out_ref):
    core = info[3]
    codes = codes_ref[...].astype(F32)
    mass = mass_ref[...]
    ones = jnp.ones_like(mass)
    for z in range(NZ):
        out_ref[z, 0:8, :] = codes
        out_ref[z, 8:9, :] = mass
        for j in range(6):
            out_ref[z, 9 + j : 10 + j, :] = vectors_ref[pl.ds(12 * z + 6 * core + j, 1), :]
        out_ref[z, 15:16, :] = ones


def joint_kernel(info, msg_ref, out_ref, hot, near, far, right):
    step = pl.program_id(0)
    z = info[1]
    core = info[3]
    rows = msg_ref.shape[2]

    @pl.when(step == 0)
    def _():
        near[...] = jnp.zeros_like(near)
        far[...] = jnp.zeros_like(far)
        right[...] = jnp.zeros_like(right)

    level = lax.broadcasted_iota(jnp.int32, (K, rows), 0).astype(F32).astype(BF16)
    for book in range(M):
        code = msg_ref[0, book : book + 1, :].astype(BF16)
        hot[book] = jnp.where(level == code, jnp.ones((), BF16), jnp.zeros((), BF16))
    mass = msg_ref[0, 8:9, :]
    weighted = msg_ref[0, 8:16, :] * mass
    hi, mid, lo = split3(weighted)
    sums = jnp.concatenate([hi, mid, lo, jnp.zeros_like(lo)], axis=0).astype(BF16)
    mass = mass.astype(BF16)
    base = pl.multiple_of(128 * core, 128)
    mine = hot[z, pl.ds(base, 128), :] * mass
    for s in range(M):
        book = (z + s) & 7
        second = hot[book]
        if 1 <= s <= 3:
            near[s - 1] += dot(mine, second, NT)
        right[book] += dot(sums, second, NT)
    low = z & 3
    side = pl.multiple_of(128 * (z >> 2), 128)
    first = hot[low, pl.ds(base, 128), :] * mass
    far[...] += dot(first, hot[low + 4, pl.ds(side, 128), :], NT)

    @pl.when(step == pl.num_programs(0) - 1)
    def _():
        for s in range(3):
            for h in range(2):
                t = 2 * s + h
                out_ref[2 * t] = near[s, 0:64, 128 * h : 128 * h + 128]
                out_ref[2 * t + 1] = near[s, 64:128, 128 * h : 128 * h + 128]
        out_ref[12] = far[0:64, :]
        out_ref[13] = far[64:128, :]
        for book in range(M):
            part = right[book]
            part = part[0:8] + part[8:16] + part[16:24]
            for h in range(2):
                i = 2 * book + h
                out_ref[14 + i // 8, 8 * (i % 8) : 8 * (i % 8) + 8, :] = part[:, 128 * h : 128 * h + 128]


def sum_kernel(in_ref, out_ref):
    total = in_ref[0]
    for i in range(1, in_ref.shape[0]):
        total = total + in_ref[i]
    for i in range(out_ref.shape[0]):
        out_ref[i] = total


def solve_kernel(places, info, ridge, *refs):
    n = len(places)
    pieces = refs[:n]
    out_ref, mass_ref = refs[n : n + 2]
    slab, high, low, wide, vec, sem = refs[n + 2 :]
    y, z, x, core = (info[i] for i in range(4))
    copies = []
    for piece, (other, parts) in zip(pieces, places):
        at_core = 1 - core if other else core
        for at, half, dy, dx, sub, size in parts:
            chunk = ((y + dy) & 3) * 4 + ((x + dx) & 3)
            row = pl.multiple_of(64 * chunk + 32 * half, 32)
            copies.append(
                pltpu.make_async_copy(
                    piece.at[pl.ds(at, size)],
                    slab.at[at_core, pl.ds(sub, size), pl.ds(row, 32), :],
                    sem,
                )
            )
    for copy in copies:
        copy.start()
    for copy in copies:
        copy.wait()

    def keep(block, r, c, tile):
        hi = tile.astype(BF16)
        high[block, r : r + 128, c : c + 128] = hi
        low[block, r : r + 128, c : c + 128] = (tile - hi.astype(F32)).astype(BF16)

    def build(p, _):
        for s in range(3):
            for h in range(2):
                for c in range(2):
                    keep(3 * p + s, 128 * c, 128 * h, slab[c, p, 128 * (2 * s + h) : 128 * (2 * s + h) + 128, :])
        return 0

    lax.fori_loop(0, M, build, 0)

    def build_far(p, _):
        for c in range(2):
            keep(24 + p, 128 * c, 0, slab[c, p, 768:896, :])
            keep(24 + p, 128 * c, 128, slab[c, p + 4, 768:896, :])
        return 0

    lax.fori_loop(0, 4, build_far, 0)

    group = 4 * y + x
    start, remain, direction, precond = 0, 1, 2, 3
    for i in range(16):
        tile = slab[group & 1, group >> 1, 896 + 8 * i : 904 + 8 * i, :]
        vec[remain, :, 128 * i : 128 * i + 128] = tile
    counts = vec[remain, 7:8, :]
    mass = jnp.sum(counts[:, 0:K], axis=1, keepdims=True)
    mass_ref[...] = jnp.broadcast_to(mass, mass_ref.shape)
    lam = ridge[0] * mass / K
    vec[precond] = jnp.broadcast_to(counts + lam, vec.shape[1:])
    vec[start] = jnp.zeros(vec.shape[1:], F32)
    scaled = vec[remain] / vec[precond]
    vec[direction] = scaled
    first_inner = jnp.sum(vec[remain] * scaled, axis=1, keepdims=True)

    def step(_, inner):
        d = vec[direction]
        hi, mid, lo = split3(d)
        wide[...] = jnp.concatenate([hi, mid, lo, jnp.zeros_like(lo)], axis=0).astype(BF16)
        image = []
        for m in range(M):
            total = jnp.zeros((32, K), F32)
            for s in range(1, M):
                q = (m + s) % M
                if s <= 3 or (s == 4 and m < 4):
                    block, dims = (3 * m + s - 1 if s <= 3 else 24 + m), NT
                else:
                    block, dims = (3 * q + 7 - s if s >= 5 else 24 + q), NN
                part = wide[:, K * q : K * q + K]
                total = total + dot(part, high[block], dims) + dot(part, low[block], dims)
            image.append(total[0:8] + total[8:16] + total[16:24])
        image = jnp.concatenate(image, axis=1) + vec[precond] * d
        alpha = inner / jnp.sum(d * image, axis=1, keepdims=True)
        vec[start] = vec[start] + alpha * d
        r = vec[remain] - alpha * image
        vec[remain] = r
        scaled = r / vec[precond]
        fresh = jnp.sum(r * scaled, axis=1, keepdims=True)
        vec[direction] = scaled + fresh / inner * d
        return fresh

    lax.fori_loop(0, ITERS, step, first_inner)
    for i in range(16):
        out_ref[6 * i : 6 * i + 6, :] = vec[start, 1:7, 128 * i : 128 * i + 128]


def residual_kernel(books_ref, codes_ref, mass_ref, vectors_ref, out_ref, table_ref, part_ref, left, hot):
    step = pl.program_id(0)

    @pl.when(step == 0)
    def _():
        for m in range(M):
            for h in range(2):
                for k in range(16):
                    i = 2 * m + h
                    table_ref[m, 6 * k : 6 * k + 6, 128 * h : 128 * h + 128] = books_ref[k, 6 * i : 6 * i + 6, :]
        for m in range(M):
            for t, piece in enumerate(split3(table_ref[m])):
                left[D * t : D * t + D, K * m : K * m + K] = piece.astype(BF16)
        part_ref[...] = jnp.zeros_like(part_ref)

    cols = codes_ref.shape[1]
    level = lax.broadcasted_iota(jnp.int32, (K, cols), 0).astype(F32).astype(BF16)
    for m in range(M):
        code = codes_ref[m : m + 1, :].astype(F32).astype(BF16)
        hot[K * m : K * m + K, :] = jnp.where(level == code, jnp.ones((), BF16), jnp.zeros((), BF16))
    recon = dot(left[...], hot[...], NN)
    recon = recon[0:D] + recon[D : 2 * D] + recon[2 * D : 3 * D]
    residual = vectors_ref[...] - recon
    out_ref[...] = residual
    total = jnp.sum(residual * residual, axis=0, keepdims=True) * mass_ref[...]
    part_ref[...] += jnp.broadcast_to(jnp.sum(total, axis=1, keepdims=True), part_ref.shape)


def shift(array, axis, by):
    size = lax.axis_size(axis)
    return lax.ppermute(array, axis, [(i, (i + by) % size) for i in range(size)])


def swap(array):
    return lax.ppermute(array, "c", [(0, 1), (1, 0)])


def ring(array, axis):
    up = shift(array, axis, 1)
    down = shift(array, axis, -1)
    half = array.shape[0] // 2
    return up, down, shift(up[:half], axis, 1), shift(down[half:], axis, -1)


def spread(array, axes):
    return lax.all_to_all(array, axes, 0, 0, tiled=True)


def body(vectors, codes, weights, ridge):
    rows = vectors.shape[0]
    vectors = vectors.T
    codes = codes.T
    mass = weights.astype(F32).reshape(1, rows)
    info = jnp.stack([lax.axis_index(a) for a in ("y", "z", "x", "c")]).astype(jnp.int32)
    message = pl.pallas_call(
        message_kernel,
        out_shape=jax.ShapeDtypeStruct((NZ, 16, rows), F32),
        in_specs=[SMEM, VMEM, VMEM, VMEM],
        out_specs=VMEM,
        compiler_params=params(),
        name="message",
    )(info, codes, mass, vectors)
    message = spread(message, "z")
    slab = pl.pallas_call(
        joint_kernel,
        grid=(NZ,),
        out_shape=jax.ShapeDtypeStruct((16, 64, 128), F32),
        in_specs=[SMEM, pl.BlockSpec((1, 16, rows), lambda i: (i, 0, 0))],
        out_specs=pl.BlockSpec((16, 64, 128), lambda i: (0, 0, 0)),
        scratch_shapes=[
            pltpu.VMEM((M, K, rows), BF16),
            pltpu.VMEM((3, 128, K), F32),
            pltpu.VMEM((128, 128), F32),
            pltpu.VMEM((M, 32, K), F32),
        ],
        compiler_params=params(dimension_semantics=("arbitrary",)),
        name="joint",
    )(info, message)
    slab = spread(slab, ("y", "x"))
    chunk = pl.pallas_call(
        sum_kernel,
        out_shape=jax.ShapeDtypeStruct((NZ, 64, 128), F32),
        in_specs=[VMEM],
        out_specs=VMEM,
        compiler_params=params(),
        name="chunk",
    )(slab)
    line = spread(chunk, "z")
    pieces = []
    for half, first, second in ((0, "y", "x"), (1, "x", "y")):
        own = line[:, 32 * half : 32 * half + 32]
        wide = jnp.concatenate([own, *ring(own, first)], axis=0)
        pieces.extend(zip(("own", "up", "down", "far0", "far1"), (half,) * 5, (wide, *ring(wide, second))))
    places, arrays = [], []
    for name, half, array in pieces:
        parts = []
        units = {"far0": (0, 1), "far1": (2, 3)}.get(name, (0, 1, 2, 3))
        outer = {"own": 0, "up": -1, "down": 1}.get(name, 2)
        for n, u in enumerate(units):
            inner = (0, -1, 1, 2)[u]
            dy, dx = (inner, outer) if half == 0 else (outer, inner)
            parts.append((8 * n, half, dy, dx, 0, 8))
        for other in (False, True):
            places.append((other, parts))
            arrays.append(swap(array) if other else array)
    columns, total_mass = pl.pallas_call(
        functools.partial(solve_kernel, places),
        out_shape=(jax.ShapeDtypeStruct((D, 128), F32), jax.ShapeDtypeStruct((8, 128), F32)),
        in_specs=[SMEM, SMEM] + [ANY] * len(arrays),
        out_specs=(VMEM, VMEM),
        scratch_shapes=[
            pltpu.VMEM((2, NZ, 1024, 128), F32),
            pltpu.VMEM((28, K, K), BF16),
            pltpu.VMEM((28, K, K), BF16),
            pltpu.VMEM((32, M * K), BF16),
            pltpu.VMEM((4, 8, M * K), F32),
            pltpu.SemaphoreType.DMA,
        ],
        compiler_params=params(),
        name="solve",
    )(info, ridge, *arrays)
    books = spread(jnp.broadcast_to(columns[None], (16, D, 128)), ("y", "x"))
    lanes = 256
    residual, table, part = pl.pallas_call(
        residual_kernel,
        grid=(rows // lanes,),
        out_shape=(
            jax.ShapeDtypeStruct((D, rows), F32),
            jax.ShapeDtypeStruct((M, D, K), F32),
            jax.ShapeDtypeStruct((8, 128), F32),
        ),
        in_specs=[
            pl.BlockSpec((16, D, 128), lambda i: (0, 0, 0)),
            pl.BlockSpec((M, lanes), lambda i: (0, i)),
            pl.BlockSpec((1, lanes), lambda i: (0, i)),
            pl.BlockSpec((D, lanes), lambda i: (0, i)),
        ],
        out_specs=(
            pl.BlockSpec((D, lanes), lambda i: (0, i)),
            pl.BlockSpec((M, D, K), lambda i: (0, 0, 0)),
            pl.BlockSpec((8, 128), lambda i: (0, 0)),
        ),
        scratch_shapes=[pltpu.VMEM((3 * D, M * K), BF16), pltpu.VMEM((M * K, lanes), BF16)],
        compiler_params=params(dimension_semantics=("arbitrary",)),
        name="residual",
    )(books, codes, mass, vectors)
    plane = spread(jnp.broadcast_to(part[:1], (16, 128)), ("y", "x"))
    plane = jnp.sum(plane, axis=0, keepdims=True)
    total = spread(jnp.broadcast_to(plane, (NZ, 128)), "z")
    total = jnp.sum(total[:, 0])
    distortion = total / (total_mass[0, 0] * D)
    return (table.transpose(0, 2, 1), residual.T, distortion)


def solution(mesh):
    finer = Mesh(mesh.devices.reshape(NY, NZ, NX, 2), ("y", "z", "x", "c"))
    placed = (P(DP, None), P(DP, None), P(DP), P())
    return jax.shard_map(
        body, mesh=finer, in_specs=placed, out_specs=(P(), P(DP, None), P()), check_vma=False
    )
```

```python
import functools

import jax
import jax.numpy as jnp
from jax import lax
from jax.experimental import pallas as pl
from jax.experimental.pallas import tpu as pltpu
from jax.sharding import Mesh
from jax.sharding import PartitionSpec as P

K = 256
M = 8
D = 96
ITERS = 8
NY, NZ, NX = 4, 8, 4
DP = ("y", "z", "x")
F32 = jnp.float32
BF16 = jnp.bfloat16
NT = (((1,), (1,)), ((), ()))
NN = (((1,), (0,)), ((), ()))


def dot(a, b, dims):
    return lax.dot_general(a, b, dims, preferred_element_type=F32)


def split3(a):
    hi = a.astype(BF16).astype(F32)
    rest = a - hi
    mid = rest.astype(BF16).astype(F32)
    return hi, mid, rest - mid


def params(**more):
    return pltpu.CompilerParams(vmem_limit_bytes=48 << 20, **more)


VMEM = pl.BlockSpec(memory_space=pltpu.VMEM)
SMEM = pl.BlockSpec(memory_space=pltpu.SMEM)
ANY = pl.BlockSpec(memory_space=pl.ANY)


def message_kernel(info, codes_ref, mass_ref, vectors_ref, out_ref):
    core = info[3]
    codes = codes_ref[...].astype(F32)
    mass = mass_ref[...]
    ones = jnp.ones_like(mass)
    for z in range(NZ):
        out_ref[z, 0:8, :] = codes
        out_ref[z, 8:9, :] = mass
        for j in range(6):
            out_ref[z, 9 + j : 10 + j, :] = vectors_ref[pl.ds(12 * z + 6 * core + j, 1), :]
        out_ref[z, 15:16, :] = ones


def joint_kernel(info, msg_ref, out_ref, hot, near, far, right, square):
    step = pl.program_id(0)
    z = info[1]
    core = info[3]
    rows = msg_ref.shape[2]

    @pl.when(step == 0)
    def _():
        near[...] = jnp.zeros_like(near)
        far[...] = jnp.zeros_like(far)
        right[...] = jnp.zeros_like(right)
        square[...] = jnp.zeros_like(square)

    level = lax.broadcasted_iota(jnp.int32, (K, rows), 0).astype(F32).astype(BF16)
    for book in range(M):
        code = msg_ref[0, book : book + 1, :].astype(BF16)
        hot[book] = jnp.where(level == code, jnp.ones((), BF16), jnp.zeros((), BF16))
    mass = msg_ref[0, 8:9, :]
    weighted = msg_ref[0, 8:16, :] * mass
    squares = weighted * msg_ref[0, 8:16, :]
    square[...] += sum(squares[:, 128 * i : 128 * i + 128] for i in range(rows // 128))
    hi, mid, lo = split3(weighted)
    sums = jnp.concatenate([hi, mid, lo, jnp.zeros_like(lo)], axis=0).astype(BF16)
    mass = mass.astype(BF16)
    base = pl.multiple_of(128 * core, 128)
    mine = hot[z, pl.ds(base, 128), :] * mass
    for s in range(M):
        book = (z + s) & 7
        second = hot[book]
        if 1 <= s <= 3:
            near[s - 1] += dot(mine, second, NT)
        right[book] += dot(sums, second, NT)
    low = z & 3
    side = pl.multiple_of(128 * (z >> 2), 128)
    first = hot[low, pl.ds(base, 128), :] * mass
    far[...] += dot(first, hot[low + 4, pl.ds(side, 128), :], NT)

    @pl.when(step == pl.num_programs(0) - 1)
    def _():
        for s in range(3):
            for h in range(2):
                t = 2 * s + h
                out_ref[2 * t] = near[s, 0:64, 128 * h : 128 * h + 128]
                out_ref[2 * t + 1] = near[s, 64:128, 128 * h : 128 * h + 128]
        out_ref[12] = far[0:64, :]
        out_ref[13] = far[64:128, :]
        for book in range(M):
            part = right[book]
            part = part[0:8] + part[8:16] + part[16:24]
            for h in range(2):
                i = 2 * book + h
                out_ref[14 + i // 8, 8 * (i % 8) : 8 * (i % 8) + 8, :] = part[:, 128 * h : 128 * h + 128]
        for j in range(6):
            out_ref[14, 8 * j : 8 * j + 1, :] = square[1 + j : 2 + j, :]


def sum_kernel(in_ref, out_ref):
    total = in_ref[0]
    for i in range(1, in_ref.shape[0]):
        total = total + in_ref[i]
    for i in range(NZ):
        for h in range(2):
            out_ref[2 * i + h] = total[32 * h : 32 * h + 32]


def solve_kernel(places, info, ridge, *refs):
    n = len(places)
    pieces = refs[:n]
    out_ref, mass_ref = refs[n : n + 2]
    slab, high, low, wide, vec, square, sem = refs[n + 2 :]
    y, z, x, core = (info[i] for i in range(4))
    copies = []
    for piece, (other, parts) in zip(pieces, places):
        holder = 1 - core if other else core
        for at, inner, outer in parts:
            dy = inner + holder * (outer - inner)
            dx = outer + holder * (inner - outer)
            chunk = ((y + dy) & 3) * 4 + ((x + dx) & 3)
            row = pl.multiple_of(64 * chunk + 32 * holder, 32)
            copies.append(
                pltpu.make_async_copy(piece.at[pl.ds(at, 16)], slab.at[:, pl.ds(row, 32), :], sem)
            )
    for copy in copies:
        copy.start()
    for copy in copies:
        copy.wait()

    def keep(block, r, c, tile):
        hi = tile.astype(BF16)
        high[block, r : r + 128, c : c + 128] = hi
        low[block, r : r + 128, c : c + 128] = (tile - hi.astype(F32)).astype(BF16)

    def build(p, _):
        for s in range(3):
            for h in range(2):
                for c in range(2):
                    keep(3 * p + s, 128 * c, 128 * h, slab[2 * p + c, 128 * (2 * s + h) : 128 * (2 * s + h) + 128, :])
        return 0

    lax.fori_loop(0, M, build, 0)

    def build_far(p, _):
        for c in range(2):
            keep(24 + p, 128 * c, 0, slab[2 * p + c, 768:896, :])
            keep(24 + p, 128 * c, 128, slab[2 * p + 8 + c, 768:896, :])
        return 0

    lax.fori_loop(0, 4, build_far, 0)

    group = 4 * y + x
    start, remain, direction, precond, right = 0, 1, 2, 3, 4
    square[...] = jnp.zeros_like(square)
    for i in range(16):
        tile = slab[group, 896 + 8 * i : 904 + 8 * i, :]
        vec[remain, :, 128 * i : 128 * i + 128] = tile
        vec[right, :, 128 * i : 128 * i + 128] = tile
        if i < 6:
            square[1 + i : 2 + i, :] = tile[0:1]
    counts = vec[remain, 7:8, :]
    mass = jnp.sum(counts[:, 0:K], axis=1, keepdims=True)
    mass_ref[...] = jnp.broadcast_to(mass, mass_ref.shape)
    lam = ridge[0] * mass / K
    vec[precond] = jnp.broadcast_to(counts + lam, vec.shape[1:])
    vec[start] = jnp.zeros(vec.shape[1:], F32)
    scaled = vec[remain] / vec[precond]
    vec[direction] = scaled
    first_inner = jnp.sum(vec[remain] * scaled, axis=1, keepdims=True)

    def operator(d):
        hi, mid, lo = split3(d)
        wide[...] = jnp.concatenate([hi, mid, lo, jnp.zeros_like(lo)], axis=0).astype(BF16)
        image = []
        for m in range(M):
            total = jnp.zeros((32, K), F32)
            for s in range(1, M):
                q = (m + s) % M
                if s <= 3 or (s == 4 and m < 4):
                    block, dims = (3 * m + s - 1 if s <= 3 else 24 + m), NT
                else:
                    block, dims = (3 * q + 7 - s if s >= 5 else 24 + q), NN
                part = wide[:, K * q : K * q + K]
                total = total + dot(part, high[block], dims) + dot(part, low[block], dims)
            image.append(total[0:8] + total[8:16] + total[16:24])
        return jnp.concatenate(image, axis=1) + vec[precond] * d

    def step(_, inner):
        d = vec[direction]
        image = operator(d)
        alpha = inner / jnp.sum(d * image, axis=1, keepdims=True)
        vec[start] = vec[start] + alpha * d
        r = vec[remain] - alpha * image
        vec[remain] = r
        scaled = r / vec[precond]
        fresh = jnp.sum(r * scaled, axis=1, keepdims=True)
        vec[direction] = scaled + fresh / inner * d
        return fresh

    lax.fori_loop(0, ITERS, step, first_inner)
    for i in range(16):
        out_ref[6 * i : 6 * i + 6, :] = vec[start, 1:7, 128 * i : 128 * i + 128]
    c = vec[start]
    fitted = c * (2.0 * vec[right] - operator(c) + lam * c)
    left = jnp.sum(square[...], axis=1, keepdims=True) - jnp.sum(fitted, axis=1, keepdims=True)
    left = jnp.sum(left[1:7], axis=0, keepdims=True)
    out_ref[96:104, :] = jnp.broadcast_to(left, (8, 128))


def residual_kernel(books_ref, mass_ref, codes_ref, vectors_ref, out_ref, table_ref, part_ref, left, hot):
    step = pl.program_id(0)

    @pl.when(step == 0)
    def _():
        for m in range(M):
            for h in range(2):
                for k in range(16):
                    i = 2 * m + h
                    table_ref[m, 6 * k : 6 * k + 6, 128 * h : 128 * h + 128] = books_ref[k, 6 * i : 6 * i + 6, :]
        for m in range(M):
            for t, piece in enumerate(split3(table_ref[m])):
                left[D * t : D * t + D, K * m : K * m + K] = piece.astype(BF16)
        total = books_ref[0, 96:97, :]
        for k in range(1, 16):
            total = total + books_ref[k, 96:97, :]
        part_ref[...] = jnp.broadcast_to(total / (mass_ref[0:1, :] * D), part_ref.shape)

    cols = codes_ref.shape[1]
    level = lax.broadcasted_iota(jnp.int32, (K, cols), 0).astype(F32).astype(BF16)
    for m in range(M):
        code = codes_ref[m : m + 1, :].astype(F32).astype(BF16)
        hot[K * m : K * m + K, :] = jnp.where(level == code, jnp.ones((), BF16), jnp.zeros((), BF16))
    recon = dot(left[...], hot[...], NN)
    recon = recon[0:D] + recon[D : 2 * D] + recon[2 * D : 3 * D]
    out_ref[...] = vectors_ref[...] - recon


def shift(array, stage, by):
    pairs = []
    for y in range(NY):
        for x in range(NX):
            for c in range(2):
                ty, tx = ((y + by) % NY, x) if (c == 0) == (stage == 0) else (y, (x + by) % NX)
                pairs.append(((y * NX + x) * 2 + c, (ty * NX + tx) * 2 + c))
    return lax.ppermute(array, ("y", "x", "c"), pairs)


def swap(array):
    return lax.ppermute(array, "c", [(0, 1), (1, 0)])


def ring(array, stage):
    up = shift(array, stage, 1)
    down = shift(array, stage, -1)
    half = array.shape[0] // 2
    return up, down, shift(up[:half], stage, 1), shift(down[half:], stage, -1)


def spread(array, axes):
    return lax.all_to_all(array, axes, 0, 0, tiled=True)


def body(vectors, codes, weights, ridge):
    rows = vectors.shape[0]
    vectors = vectors.T
    codes = codes.T
    mass = weights.astype(F32).reshape(1, rows)
    info = jnp.stack([lax.axis_index(a) for a in ("y", "z", "x", "c")]).astype(jnp.int32)
    message = pl.pallas_call(
        message_kernel,
        out_shape=jax.ShapeDtypeStruct((NZ, 16, rows), F32),
        in_specs=[SMEM, VMEM, VMEM, VMEM],
        out_specs=VMEM,
        compiler_params=params(),
        name="message",
    )(info, codes, mass, vectors)
    message = spread(message, "z")
    slab = pl.pallas_call(
        joint_kernel,
        grid=(NZ,),
        out_shape=jax.ShapeDtypeStruct((16, 64, 128), F32),
        in_specs=[SMEM, pl.BlockSpec((1, 16, rows), lambda i: (i, 0, 0))],
        out_specs=pl.BlockSpec((16, 64, 128), lambda i: (0, 0, 0)),
        scratch_shapes=[
            pltpu.VMEM((M, K, rows), BF16),
            pltpu.VMEM((3, 128, K), F32),
            pltpu.VMEM((128, 128), F32),
            pltpu.VMEM((M, 32, K), F32),
            pltpu.VMEM((8, 128), F32),
        ],
        compiler_params=params(dimension_semantics=("arbitrary",)),
        name="joint",
    )(info, message)
    slab = spread(slab, ("y", "x"))
    chunk = pl.pallas_call(
        sum_kernel,
        out_shape=jax.ShapeDtypeStruct((16, 32, 128), F32),
        in_specs=[VMEM],
        out_specs=VMEM,
        compiler_params=params(),
        name="chunk",
    )(slab)
    line = spread(chunk, ("z", "c"))
    wide = jnp.concatenate([line, *ring(line, 0)], axis=0)
    offsets = (0, -1, 1, 2)
    places, arrays = [], []
    for array, outer, units in zip(
        (wide, *ring(wide, 1)), (0, -1, 1, 2, 2), ((0, 1, 2, 3),) * 3 + ((0, 1), (2, 3))
    ):
        parts = [(16 * n, offsets[u], outer) for n, u in enumerate(units)]
        for other in (False, True):
            places.append((other, parts))
            arrays.append(swap(array) if other else array)
    columns, total_mass = pl.pallas_call(
        functools.partial(solve_kernel, places),
        out_shape=(jax.ShapeDtypeStruct((104, 128), F32), jax.ShapeDtypeStruct((8, 128), F32)),
        in_specs=[SMEM, SMEM] + [ANY] * len(arrays),
        out_specs=(VMEM, VMEM),
        scratch_shapes=[
            pltpu.VMEM((16, 1024, 128), F32),
            pltpu.VMEM((28, K, K), BF16),
            pltpu.VMEM((28, K, K), BF16),
            pltpu.VMEM((32, M * K), BF16),
            pltpu.VMEM((5, 8, M * K), F32),
            pltpu.VMEM((8, 128), F32),
            pltpu.SemaphoreType.DMA,
        ],
        compiler_params=params(),
        name="solve",
    )(info, ridge, *arrays)
    books = spread(jnp.broadcast_to(columns[None], (16, *columns.shape)), ("y", "x"))
    lanes = 256
    residual, table, part = pl.pallas_call(
        residual_kernel,
        grid=(rows // lanes,),
        out_shape=(
            jax.ShapeDtypeStruct((D, rows), F32),
            jax.ShapeDtypeStruct((M, D, K), F32),
            jax.ShapeDtypeStruct((8, 128), F32),
        ),
        in_specs=[
            pl.BlockSpec((16, 104, 128), lambda i: (0, 0, 0)),
            pl.BlockSpec((8, 128), lambda i: (0, 0)),
            pl.BlockSpec((M, lanes), lambda i: (0, i)),
            pl.BlockSpec((D, lanes), lambda i: (0, i)),
        ],
        out_specs=(
            pl.BlockSpec((D, lanes), lambda i: (0, i)),
            pl.BlockSpec((M, D, K), lambda i: (0, 0, 0)),
            pl.BlockSpec((8, 128), lambda i: (0, 0)),
        ),
        scratch_shapes=[pltpu.VMEM((3 * D, M * K), BF16), pltpu.VMEM((M * K, lanes), BF16)],
        compiler_params=params(dimension_semantics=("arbitrary",)),
        name="residual",
    )(books, total_mass, codes, vectors)
    return (table.transpose(0, 2, 1), residual.T, part[0, 0])


def solution(mesh):
    finer = Mesh(mesh.devices.reshape(NY, NZ, NX, 2), ("y", "z", "x", "c"))
    placed = (P(DP, None), P(DP, None), P(DP), P())
    return jax.shard_map(
        body, mesh=finer, in_specs=placed, out_specs=(P(), P(DP, None), P()), check_vma=False
    )
```

```python
import functools

import jax
import jax.numpy as jnp
from jax import lax
from jax.experimental import pallas as pl
from jax.experimental.pallas import tpu as pltpu
from jax.sharding import Mesh
from jax.sharding import PartitionSpec as P

K = 256
M = 8
D = 96
ITERS = 8
NY, NZ, NX = 4, 8, 4
DP = ("y", "z", "x")
F32 = jnp.float32
BF16 = jnp.bfloat16
NT = (((1,), (1,)), ((), ()))
NN = (((1,), (0,)), ((), ()))


def dot(a, b, dims):
    return lax.dot_general(a, b, dims, preferred_element_type=F32)


def split3(a):
    hi = a.astype(BF16).astype(F32)
    rest = a - hi
    mid = rest.astype(BF16).astype(F32)
    return hi, mid, rest - mid


def params(mib, **more):
    return pltpu.CompilerParams(vmem_limit_bytes=mib << 20, **more)


VMEM = pl.BlockSpec(memory_space=pltpu.VMEM)
SMEM = pl.BlockSpec(memory_space=pltpu.SMEM)
ANY = pl.BlockSpec(memory_space=pl.ANY)


def message_kernel(info, codes_ref, mass_ref, vectors_ref, *out_refs):
    z = info[1]
    core = info[3]

    def half(a):
        n = a.shape[1] // 2
        return jnp.where(core == 0, a[:, :n], a[:, n:])

    codes = codes_ref[...].astype(F32)
    mass = mass_ref[...]
    for d, out_ref in enumerate(out_refs):
        keep = half if d == 4 else (lambda a: a)
        to = (z + d * (1 - 2 * core)) & 7
        out_ref[0:8, :] = keep(codes)
        for c in range(2):
            out_ref[8 + 8 * c : 9 + 8 * c, :] = keep(mass)
            for j in range(6):
                row = keep(vectors_ref[pl.ds(12 * to + 6 * c + j, 1), :])
                out_ref[9 + 8 * c + j : 10 + 8 * c + j, :] = row
            out_ref[15 + 8 * c : 16 + 8 * c, :] = keep(jnp.ones_like(mass))


def joint_kernel(count, first, last, info, *refs):
    messages, refs = refs[:count], refs[count:]
    if not first:
        before, refs = refs[:4], refs[4:]
    if last:
        out_ref, refs = refs[0], refs[1:]
    near, far, right, square, left, *hots = refs
    z = info[1]
    core = info[3]
    for n, ref in enumerate((near, far, right, square)):
        ref[...] = jnp.zeros_like(ref) if first else before[n][...]
    wide = hots[0].shape[2]
    level = lax.broadcasted_iota(jnp.int32, (K, wide), 0).astype(F32).astype(BF16)
    low = z & 3
    levels = lax.broadcasted_iota(jnp.int32, (128, wide), 0)
    based = (levels + 128 * core).astype(F32).astype(BF16)
    sided = (levels + 128 * (z >> 2)).astype(F32).astype(BF16)
    turn = 0
    for message in messages:
        for at in range(0, message.shape[1], wide):
            hot, turn = hots[turn % 2], turn + 1
            lanes = pl.ds(at, wide)
            for s in range(M):
                code = message[pl.ds((z + s) & 7, 1), lanes].astype(BF16)
                hot[s] = jnp.where(level == code, jnp.ones((), BF16), jnp.zeros((), BF16))
            own = message[pl.ds(pl.multiple_of(8 + 8 * core, 8), 8), lanes]
            weighted = own * own_mass(message, lanes)
            squares = weighted * own
            square[...] += sum(squares[:, 128 * i : 128 * i + 128] for i in range(wide // 128))
            hi, mid, lo = split3(weighted)
            mass = own_mass(message, lanes).astype(BF16)
            part = left.at[turn % 2]
            part[0:128] = jnp.where(based == message[pl.ds(z, 1), lanes].astype(BF16), mass, jnp.zeros((), BF16))
            part[128:160] = jnp.concatenate([hi, mid, lo, jnp.zeros_like(lo)], axis=0).astype(BF16)
            part[160:288] = jnp.where(based == message[pl.ds(low, 1), lanes].astype(BF16), mass, jnp.zeros((), BF16))
            code = message[pl.ds(low + 4, 1), lanes].astype(BF16)
            part[288:416] = jnp.where(sided == code, jnp.ones((), BF16), jnp.zeros((), BF16))
            for s in range(M):
                if 1 <= s <= 3:
                    near[s - 1] += dot(part[0:160], hot[s], NT)
                else:
                    right[s] += dot(part[128:160], hot[s], NT)
            far[...] += dot(part[160:288], part[288:416], NT)
    if last:
        for s in range(3):
            for h in range(2):
                t = 2 * s + h
                out_ref[2 * t] = near[s, 0:64, 128 * h : 128 * h + 128]
                out_ref[2 * t + 1] = near[s, 64:128, 128 * h : 128 * h + 128]
        out_ref[12] = far[0:64, :]
        out_ref[13] = far[64:128, :]
        for s in range(M):
            total = near[s - 1, 128:160] if 1 <= s <= 3 else right[s]
            total = total[0:8] + total[8:16] + total[16:24]
            for h in range(2):
                i = 2 * ((z + s) & 7) + h
                row = pl.multiple_of(8 * (i & 7), 8)
                out_ref[14 + (i >> 3), pl.ds(row, 8), :] = total[:, 128 * h : 128 * h + 128]
        for j in range(6):
            out_ref[14, 8 * j : 8 * j + 1, :] = square[1 + j : 2 + j, :]


def own_mass(message, lanes):
    return message[8:9, lanes]


def joint(info, messages, before, last):
    shapes = [(3, 160, K), (128, 128), (M, 32, K), (8, 128)]
    state = [jax.ShapeDtypeStruct(a, F32) for a in shapes]
    wide = 512
    scratch = [pltpu.VMEM((2, 416, wide), BF16), pltpu.VMEM((M, K, wide), BF16), pltpu.VMEM((M, K, wide), BF16)]
    if last:
        scratch = [pltpu.VMEM(a, F32) for a in shapes] + scratch
    count = len(messages)
    return pl.pallas_call(
        functools.partial(joint_kernel, count, not before, last),
        out_shape=jax.ShapeDtypeStruct((16, 64, 128), F32) if last else state,
        in_specs=[SMEM] + [VMEM] * (count + len(before)),
        out_specs=VMEM if last else [VMEM] * 4,
        scratch_shapes=scratch,
        compiler_params=params(16),
        cost_estimate=pl.CostEstimate(flops=5 * 10**8 * count, bytes_accessed=10**6, transcendentals=0),
        name="joint",
    )(info, *messages, *before)


def sum_kernel(in_ref, out_ref):
    total = in_ref[0]
    for i in range(1, in_ref.shape[0]):
        total = total + in_ref[i]
    for i in range(NZ):
        out_ref[i] = total


OFFSETS = (0, -1, 1, 2)


def position(info, holder, inner, outer):
    dy = inner + holder * (outer - inner)
    dx = outer + holder * (inner - outer)
    return ((info[0] + dy) & 3) * 4 + ((info[2] + dx) & 3)


def solve_kernel(places, info, ridge, *refs):
    n = len(places)
    pieces = refs[:n]
    out_ref, mass_ref = refs[n : n + 2]
    slab, high, low, wide, vec, square, result = refs[n + 2 :]
    core = info[3]
    for piece, (other, parts) in zip(pieces, places):
        holder = 1 - core if other else core
        for at, inner, outer in parts:
            row = pl.multiple_of(64 * position(info, holder, inner, outer), 64)
            for z in range(NZ):
                slab[2 * z + holder, pl.ds(row, 64), :] = piece[at + z]

    def keep(m, r, c, tile):
        hi = tile.astype(BF16)
        high[m, r : r + 128, c : c + 128] = hi
        low[m, r : r + 128, c : c + 128] = (tile - hi.astype(F32)).astype(BF16)

    def build(p, _):
        for s in range(1, 4):
            for h in range(2):
                for c in range(2):
                    tile = slab[2 * p + c, 128 * (2 * s - 2 + h) : 128 * (2 * s - 1 + h), :]
                    keep((p + s) & 7, K * (7 - s) + 128 * c, 128 * h, tile)
                    keep(p, K * (s - 1) + 128 * h, 128 * c, tile.T)
        return 0

    lax.fori_loop(0, M, build, 0)

    def build_far(p, _):
        for h in range(2):
            for c in range(2):
                tile = slab[2 * p + 8 * h + c, 768:896, :]
                keep(p + 4, 3 * K + 128 * c, 128 * h, tile)
                keep(p, 3 * K + 128 * h, 128 * c, tile.T)
        return 0

    lax.fori_loop(0, 4, build_far, 0)

    group = 4 * info[0] + info[2]
    start, remain, direction, precond, inverse, right = range(6)
    square[...] = jnp.zeros_like(square)
    for i in range(16):
        tile = slab[group, 896 + 8 * i : 904 + 8 * i, :]
        vec[remain, :, 128 * i : 128 * i + 128] = tile
        vec[right, :, 128 * i : 128 * i + 128] = tile
        if i < 6:
            square[1 + i : 2 + i, :] = tile[0:1]
    counts = vec[remain, 7:8, :]
    mass = jnp.sum(counts[:, 0:K], axis=1, keepdims=True)
    mass_ref[...] = jnp.broadcast_to(mass, mass_ref.shape)
    lam = ridge[0] * mass / K
    vec[precond] = jnp.broadcast_to(counts + lam, vec.shape[1:])
    vec[inverse] = jnp.broadcast_to(1.0 / (counts + lam), vec.shape[1:])
    vec[start] = jnp.zeros(vec.shape[1:], F32)
    scaled = vec[remain] * vec[inverse]
    vec[direction] = scaled
    first_inner = jnp.sum(vec[remain] * scaled, axis=1, keepdims=True)

    def operator(d):
        pieces = jnp.concatenate(split3(d), axis=0).astype(BF16)
        wide[:, 0 : M * K] = pieces
        wide[:, M * K :] = pieces
        image = []
        for m in range(M):
            part = wide[:, K * (m + 1) : K * (m + 8)]
            total = dot(part, high[m], NN) + dot(part, low[m], NN)
            image.append(total[0:8] + total[8:16] + total[16:24])
        return jnp.concatenate(image, axis=1) + vec[precond] * d

    def step(_, inner):
        d = vec[direction]
        image = operator(d)
        alpha = inner / jnp.sum(d * image, axis=1, keepdims=True)
        vec[start] = vec[start] + alpha * d
        r = vec[remain] - alpha * image
        vec[remain] = r
        scaled = r * vec[inverse]
        fresh = jnp.sum(r * scaled, axis=1, keepdims=True)
        vec[direction] = scaled + fresh / inner * d
        return fresh

    lax.fori_loop(0, ITERS, step, first_inner)
    for i in range(16):
        result[6 * i : 6 * i + 6, :] = vec[start, 1:7, 128 * i : 128 * i + 128]
    c = vec[start]
    fitted = c * (vec[right] + vec[remain] + lam * c)
    left = jnp.sum(square[...], axis=1, keepdims=True) - jnp.sum(fitted, axis=1, keepdims=True)
    left = jnp.sum(left[1:7], axis=0, keepdims=True)
    result[96:112, :] = jnp.broadcast_to(left, (16, 128))
    out_ref[...] = result[pl.ds(pl.multiple_of(56 * core, 8), 56), :]


def residual_kernel(
    info, wide_ref, rest_ref, wide_other, rest_other, mass_ref, codes_ref, vectors_ref,
    out_ref, table_ref, part_ref, left, hot, books_ref,
):
    step = pl.program_id(0)

    @pl.when(step == 0)
    def _():
        core = info[3]
        for holder, first, second in ((core, wide_ref, rest_ref), (1 - core, wide_other, rest_other)):
            row = pl.multiple_of(56 * holder, 8)
            for u in range(16):
                k = position(info, holder, OFFSETS[u % 4], OFFSETS[u // 4])
                books_ref[k, pl.ds(row, 56), :] = first[u] if u < 4 else second[u - 4]
        for m in range(M):
            for h in range(2):
                for k in range(16):
                    i = 2 * m + h
                    table_ref[m, 6 * k : 6 * k + 6, 128 * h : 128 * h + 128] = books_ref[k, 6 * i : 6 * i + 6, :]
        for m in range(M):
            for t, piece in enumerate(split3(table_ref[m])):
                left[D * t : D * t + D, K * m : K * m + K] = piece.astype(BF16)
        total = books_ref[0, 96:97, :]
        for k in range(1, 16):
            total = total + books_ref[k, 96:97, :]
        part_ref[...] = jnp.broadcast_to(total / (mass_ref[0:1, :] * D), part_ref.shape)

    cols = codes_ref.shape[1]
    level = lax.broadcasted_iota(jnp.int32, (K, cols), 0).astype(F32).astype(BF16)
    for m in range(M):
        code = codes_ref[m : m + 1, :].astype(F32).astype(BF16)
        hot[K * m : K * m + K, :] = jnp.where(level == code, jnp.ones((), BF16), jnp.zeros((), BF16))
    recon = dot(left[...], hot[...], NN)
    recon = recon[0:D] + recon[D : 2 * D] + recon[2 * D : 3 * D]
    out_ref[...] = vectors_ref[...] - recon


def shift(array, stage, by):
    pairs = []
    for y in range(NY):
        for x in range(NX):
            for c in range(2):
                ty, tx = ((y + by) % NY, x) if (c == 0) == (stage == 0) else (y, (x + by) % NX)
                pairs.append(((y * NX + x) * 2 + c, (ty * NX + tx) * 2 + c))
    return lax.ppermute(array, ("y", "x", "c"), pairs)


def swap(array):
    return lax.ppermute(array, "c", [(0, 1), (1, 0)])


def ring(array, stage):
    up = shift(array, stage, 1)
    down = shift(array, stage, -1)
    half = array.shape[0] // 2
    return up, down, shift(up[:half], stage, 1), shift(down[half:], stage, -1)


def along_z(array, by):
    pairs = []
    for z in range(NZ):
        for c in range(2):
            pairs.append((2 * z + c, 2 * ((z + by * (1 - 2 * c)) % NZ) + c))
    return lax.ppermute(array, ("z", "c"), pairs)


def spread(array, axes):
    return lax.all_to_all(array, axes, 0, 0, tiled=True)


def body(vectors, codes, weights, ridge):
    rows = vectors.shape[0]
    vectors = vectors.T
    codes = codes.T
    mass = weights.astype(F32).reshape(1, rows)
    info = jnp.stack([lax.axis_index(a) for a in ("y", "z", "x", "c")]).astype(jnp.int32)
    own, *messages = pl.pallas_call(
        message_kernel,
        out_shape=[jax.ShapeDtypeStruct((24, rows if d < 4 else rows // 2), F32) for d in range(5)],
        in_specs=[SMEM, VMEM, VMEM, VMEM],
        out_specs=[VMEM] * 5,
        compiler_params=params(16),
        name="message",
    )(info, codes, mass, vectors)
    messages = [along_z(message, d + 1) for d, message in enumerate(messages)]
    state = joint(info, [own], [], False)
    others = [swap(message) for message in messages]
    state = joint(info, messages, state, False)
    slab = joint(info, others, state, True)
    slab = spread(slab, ("y", "x"))
    chunk = pl.pallas_call(
        sum_kernel,
        out_shape=jax.ShapeDtypeStruct((NZ, 64, 128), F32),
        in_specs=[VMEM],
        out_specs=VMEM,
        compiler_params=params(8),
        name="chunk",
    )(slab)
    line = spread(chunk, "z")
    wide = jnp.concatenate([line, *ring(line, 0)], axis=0)
    places, arrays = [], []
    for array, outer, units in zip(
        (wide, *ring(wide, 1)), (0, -1, 1, 2, 2), ((0, 1, 2, 3),) * 3 + ((0, 1), (2, 3))
    ):
        parts = [(8 * n, OFFSETS[u], outer) for n, u in enumerate(units)]
        for other in (False, True):
            places.append((other, parts))
            arrays.append(swap(array) if other else array)
    columns, total_mass = pl.pallas_call(
        functools.partial(solve_kernel, places),
        out_shape=(jax.ShapeDtypeStruct((56, 128), F32), jax.ShapeDtypeStruct((8, 128), F32)),
        in_specs=[SMEM, SMEM] + [VMEM] * len(arrays),
        out_specs=(VMEM, VMEM),
        scratch_shapes=[
            pltpu.VMEM((16, 1024, 128), F32),
            pltpu.VMEM((M, 7 * K, K), BF16),
            pltpu.VMEM((M, 7 * K, K), BF16),
            pltpu.VMEM((24, 2 * M * K), BF16),
            pltpu.VMEM((6, 8, M * K), F32),
            pltpu.VMEM((8, 128), F32),
            pltpu.VMEM((112, 128), F32),
        ],
        compiler_params=params(40),
        name="solve",
    )(info, ridge, *arrays)
    wide = jnp.stack([columns] + [shift(columns, 0, by) for by in (1, -1, 2)])
    rest = jnp.concatenate([shift(wide, 1, by) for by in (1, -1, 2)], axis=0)
    lanes = 256
    residual, table, part = pl.pallas_call(
        residual_kernel,
        grid=(rows // lanes,),
        out_shape=(
            jax.ShapeDtypeStruct((D, rows), F32),
            jax.ShapeDtypeStruct((M, D, K), F32),
            jax.ShapeDtypeStruct((8, 128), F32),
        ),
        in_specs=[
            SMEM,
            pl.BlockSpec((4, 56, 128), lambda i: (0, 0, 0)),
            pl.BlockSpec((12, 56, 128), lambda i: (0, 0, 0)),
            pl.BlockSpec((4, 56, 128), lambda i: (0, 0, 0)),
            pl.BlockSpec((12, 56, 128), lambda i: (0, 0, 0)),
            pl.BlockSpec((8, 128), lambda i: (0, 0)),
            pl.BlockSpec((M, lanes), lambda i: (0, i)),
            pl.BlockSpec((D, lanes), lambda i: (0, i)),
        ],
        out_specs=(
            pl.BlockSpec((D, lanes), lambda i: (0, i)),
            pl.BlockSpec((M, D, K), lambda i: (0, 0, 0)),
            pl.BlockSpec((8, 128), lambda i: (0, 0)),
        ),
        scratch_shapes=[
            pltpu.VMEM((3 * D, M * K), BF16),
            pltpu.VMEM((M * K, lanes), BF16),
            pltpu.VMEM((16, 112, 128), F32),
        ],
        compiler_params=params(24, dimension_semantics=("arbitrary",)),
        name="residual",
    )(info, wide, rest, swap(wide), swap(rest), total_mass, codes, vectors)
    return (table.transpose(0, 2, 1), residual.T, part[0, 0])


def solution(mesh):
    finer = Mesh(mesh.devices.reshape(NY, NZ, NX, 2), ("y", "z", "x", "c"))
    placed = (P(DP, None), P(DP, None), P(DP), P())
    return jax.shard_map(
        body, mesh=finer, in_specs=placed, out_specs=(P(), P(DP, None), P()), check_vma=False
    )
```

```python
import functools

import jax
import jax.numpy as jnp
from jax import lax
from jax.experimental import pallas as pl
from jax.experimental.pallas import tpu as pltpu
from jax.sharding import Mesh
from jax.sharding import PartitionSpec as P

K = 256
M = 8
D = 96
ITERS = 8
NY, NZ, NX = 4, 8, 4
DP = ("y", "z", "x")
F32 = jnp.float32
BF16 = jnp.bfloat16
NT = (((1,), (1,)), ((), ()))
NN = (((1,), (0,)), ((), ()))


def dot(a, b, dims):
    return lax.dot_general(a, b, dims, preferred_element_type=F32)


def split3(a):
    hi = a.astype(BF16).astype(F32)
    rest = a - hi
    mid = rest.astype(BF16).astype(F32)
    return hi, mid, rest - mid


def params(mib, **more):
    return pltpu.CompilerParams(vmem_limit_bytes=mib << 20, **more)


VMEM = pl.BlockSpec(memory_space=pltpu.VMEM)
SMEM = pl.BlockSpec(memory_space=pltpu.SMEM)
ANY = pl.BlockSpec(memory_space=pl.ANY)


def message_kernel(info, codes_ref, mass_ref, vectors_ref, *out_refs):
    z = info[1]
    core = info[3]

    def half(a):
        n = a.shape[1] // 2
        return jnp.where(core == 0, a[:, :n], a[:, n:])

    codes = codes_ref[...].astype(F32)
    mass = mass_ref[...]
    for d, out_ref in enumerate(out_refs):
        keep = half if d == 4 else (lambda a: a)
        to = (z + d * (1 - 2 * core)) & 7
        out_ref[0:8, :] = keep(codes)
        for c in range(2):
            out_ref[8 + 8 * c : 9 + 8 * c, :] = keep(mass)
            for j in range(6):
                row = keep(vectors_ref[pl.ds(12 * to + 6 * c + j, 1), :])
                out_ref[9 + 8 * c + j : 10 + 8 * c + j, :] = row
            out_ref[15 + 8 * c : 16 + 8 * c, :] = keep(jnp.ones_like(mass))


def joint_kernel(count, first, last, info, *refs):
    messages, refs = refs[:count], refs[count:]
    if not first:
        before, refs = refs[:4], refs[4:]
    if last:
        out_ref, refs = refs[0], refs[1:]
    near, far, right, square, left, *hots = refs
    z = info[1]
    core = info[3]
    for n, ref in enumerate((near, far, right, square)):
        ref[...] = jnp.zeros_like(ref) if first else before[n][...]
    wide = hots[0].shape[2]
    level = lax.broadcasted_iota(jnp.int32, (K, wide), 0).astype(F32).astype(BF16)
    low = z & 3
    levels = lax.broadcasted_iota(jnp.int32, (128, wide), 0)
    based = (levels + 128 * core).astype(F32).astype(BF16)
    sided = (levels + 128 * (z >> 2)).astype(F32).astype(BF16)
    turn = 0
    for message in messages:
        for at in range(0, message.shape[1], wide):
            hot, turn = hots[turn % 2], turn + 1
            lanes = pl.ds(at, wide)
            for s in range(M):
                code = message[pl.ds((z + s) & 7, 1), lanes].astype(BF16)
                hot[s] = jnp.where(level == code, jnp.ones((), BF16), jnp.zeros((), BF16))
            own = message[pl.ds(pl.multiple_of(8 + 8 * core, 8), 8), lanes]
            weighted = own * own_mass(message, lanes)
            squares = weighted * own
            square[...] += sum(squares[:, 128 * i : 128 * i + 128] for i in range(wide // 128))
            hi, mid, lo = split3(weighted)
            mass = own_mass(message, lanes).astype(BF16)
            part = left.at[turn % 2]
            part[0:128] = jnp.where(based == message[pl.ds(z, 1), lanes].astype(BF16), mass, jnp.zeros((), BF16))
            part[128:160] = jnp.concatenate([hi, mid, lo, jnp.zeros_like(lo)], axis=0).astype(BF16)
            part[160:288] = jnp.where(based == message[pl.ds(low, 1), lanes].astype(BF16), mass, jnp.zeros((), BF16))
            code = message[pl.ds(low + 4, 1), lanes].astype(BF16)
            part[288:416] = jnp.where(sided == code, jnp.ones((), BF16), jnp.zeros((), BF16))
            for s in range(M):
                if 1 <= s <= 3:
                    near[s - 1] += dot(part[0:160], hot[s], NT)
                else:
                    right[s] += dot(part[128:160], hot[s], NT)
            far[...] += dot(part[160:288], part[288:416], NT)
    if last:
        for s in range(3):
            for h in range(2):
                t = 2 * s + h
                out_ref[2 * t] = near[s, 0:64, 128 * h : 128 * h + 128]
                out_ref[2 * t + 1] = near[s, 64:128, 128 * h : 128 * h + 128]
        out_ref[12] = far[0:64, :]
        out_ref[13] = far[64:128, :]
        for s in range(M):
            total = near[s - 1, 128:160] if 1 <= s <= 3 else right[s]
            total = total[0:8] + total[8:16] + total[16:24]
            for h in range(2):
                i = 2 * ((z + s) & 7) + h
                row = pl.multiple_of(8 * (i & 7), 8)
                out_ref[14 + (i >> 3), pl.ds(row, 8), :] = total[:, 128 * h : 128 * h + 128]
        for j in range(6):
            out_ref[14, 8 * j : 8 * j + 1, :] = square[1 + j : 2 + j, :]


def own_mass(message, lanes):
    return message[8:9, lanes]


def joint(info, messages, before, last):
    shapes = [(3, 160, K), (128, 128), (M, 32, K), (8, 128)]
    state = [jax.ShapeDtypeStruct(a, F32) for a in shapes]
    wide = 512
    scratch = [pltpu.VMEM((2, 416, wide), BF16), pltpu.VMEM((M, K, wide), BF16), pltpu.VMEM((M, K, wide), BF16)]
    if last:
        scratch = [pltpu.VMEM(a, F32) for a in shapes] + scratch
    count = len(messages)
    return pl.pallas_call(
        functools.partial(joint_kernel, count, not before, last),
        out_shape=jax.ShapeDtypeStruct((16, 64, 128), F32) if last else state,
        in_specs=[SMEM] + [VMEM] * (count + len(before)),
        out_specs=VMEM if last else [VMEM] * 4,
        scratch_shapes=scratch,
        compiler_params=params(16),
        cost_estimate=pl.CostEstimate(flops=5 * 10**8 * count, bytes_accessed=10**6, transcendentals=0),
        name="joint",
    )(info, *messages, *before)


def sum_kernel(in_ref, out_ref):
    total = in_ref[0]
    for i in range(1, in_ref.shape[0]):
        total = total + in_ref[i]
    for i in range(NZ):
        out_ref[i] = total


OFFSETS = (0, -1, 1, 2)


def position(info, holder, inner, outer):
    dy = inner + holder * (outer - inner)
    dx = outer + holder * (inner - outer)
    return ((info[0] + dy) & 3) * 4 + ((info[2] + dx) & 3)


def solve_kernel(places, info, ridge, *refs):
    n = len(places)
    pieces = refs[:n]
    out_ref, mass_ref = refs[n : n + 2]
    slab, high, low, wide, vec, square, result = refs[n + 2 :]
    core = info[3]
    for piece, (other, parts) in zip(pieces, places):
        holder = 1 - core if other else core
        for at, inner, outer in parts:
            row = pl.multiple_of(64 * position(info, holder, inner, outer), 64)
            for z in range(NZ):
                slab[2 * z + holder, pl.ds(row, 64), :] = piece[at + z]

    def keep(m, r, c, tile):
        hi = tile.astype(BF16)
        high[m, r : r + 128, c : c + 128] = hi
        low[m, r : r + 128, c : c + 128] = (tile - hi.astype(F32)).astype(BF16)

    def build(p, _):
        for s in range(1, 4):
            for h in range(2):
                for c in range(2):
                    tile = slab[2 * p + c, 128 * (2 * s - 2 + h) : 128 * (2 * s - 1 + h), :]
                    keep((p + s) & 7, K * (7 - s) + 128 * c, 128 * h, tile)
                    keep(p, K * (s - 1) + 128 * h, 128 * c, tile.T)
        return 0

    lax.fori_loop(0, M, build, 0)

    def build_far(p, _):
        for h in range(2):
            for c in range(2):
                tile = slab[2 * p + 8 * h + c, 768:896, :]
                keep(p + 4, 3 * K + 128 * c, 128 * h, tile)
                keep(p, 3 * K + 128 * h, 128 * c, tile.T)
        return 0

    lax.fori_loop(0, 4, build_far, 0)

    group = 4 * info[0] + info[2]
    start, remain, direction, precond, inverse, right = range(6)
    square[...] = jnp.zeros_like(square)
    for i in range(16):
        tile = slab[group, 896 + 8 * i : 904 + 8 * i, :]
        vec[remain, :, 128 * i : 128 * i + 128] = tile
        vec[right, :, 128 * i : 128 * i + 128] = tile
        if i < 6:
            square[1 + i : 2 + i, :] = tile[0:1]
    counts = vec[remain, 7:8, :]
    mass = jnp.sum(counts[:, 0:K], axis=1, keepdims=True)
    mass_ref[...] = jnp.broadcast_to(mass, mass_ref.shape)
    lam = ridge[0] * mass / K
    vec[precond] = jnp.broadcast_to(counts + lam, vec.shape[1:])
    vec[inverse] = jnp.broadcast_to(1.0 / (counts + lam), vec.shape[1:])
    vec[start] = jnp.zeros(vec.shape[1:], F32)
    scaled = vec[remain] * vec[inverse]
    vec[direction] = scaled
    first_inner = jnp.sum(vec[remain] * scaled, axis=1, keepdims=True)

    def operator(d):
        pieces = jnp.concatenate(split3(d), axis=0).astype(BF16)
        wide[:, 0 : M * K] = pieces
        wide[:, M * K :] = pieces
        image = []
        for m in range(M):
            part = wide[:, K * (m + 1) : K * (m + 8)]
            total = dot(part, high[m], NN) + dot(part, low[m], NN)
            image.append(total[0:8] + total[8:16] + total[16:24])
        return jnp.concatenate(image, axis=1) + vec[precond] * d

    def step(_, inner):
        d = vec[direction]
        image = operator(d)
        alpha = inner / jnp.sum(d * image, axis=1, keepdims=True)
        vec[start] = vec[start] + alpha * d
        r = vec[remain] - alpha * image
        vec[remain] = r
        scaled = r * vec[inverse]
        fresh = jnp.sum(r * scaled, axis=1, keepdims=True)
        vec[direction] = scaled + fresh / inner * d
        return fresh

    lax.fori_loop(0, ITERS, step, first_inner)
    for i in range(16):
        result[6 * i : 6 * i + 6, :] = vec[start, 1:7, 128 * i : 128 * i + 128]
    c = vec[start]
    fitted = c * (vec[right] + vec[remain] + lam * c)
    left = jnp.sum(square[...], axis=1, keepdims=True) - jnp.sum(fitted, axis=1, keepdims=True)
    left = jnp.sum(left[1:7], axis=0, keepdims=True)
    result[96:112, :] = jnp.broadcast_to(left, (16, 128))
    out_ref[...] = result[pl.ds(pl.multiple_of(56 * core, 8), 56), :]


def residual_kernel(
    info, wide_ref, rest_ref, wide_other, rest_other, mass_ref, codes_ref, vectors_ref,
    out_ref, table_ref, part_ref, left, hot, books_ref,
):
    step = pl.program_id(0)

    @pl.when(step == 0)
    def _():
        core = info[3]
        for holder, first, second in ((core, wide_ref, rest_ref), (1 - core, wide_other, rest_other)):
            row = pl.multiple_of(56 * holder, 8)
            for u in range(16):
                k = position(info, holder, OFFSETS[u % 4], OFFSETS[u // 4])
                books_ref[k, pl.ds(row, 56), :] = first[u] if u < 4 else second[u - 4]
        for m in range(M):
            for h in range(2):
                for k in range(16):
                    i = 2 * m + h
                    table_ref[m, 6 * k : 6 * k + 6, 128 * h : 128 * h + 128] = books_ref[k, 6 * i : 6 * i + 6, :]
        for m in range(M):
            for t, piece in enumerate(split3(table_ref[m])):
                left[D * t : D * t + D, K * m : K * m + K] = piece.astype(BF16)
        total = books_ref[0, 96:97, :]
        for k in range(1, 16):
            total = total + books_ref[k, 96:97, :]
        part_ref[0] = (total / (mass_ref[0:1, :] * D))[0, 0]

    cols = codes_ref.shape[1]
    level = lax.broadcasted_iota(jnp.int32, (K, cols), 0).astype(F32).astype(BF16)
    for m in range(M):
        code = codes_ref[m : m + 1, :].astype(F32).astype(BF16)
        hot[K * m : K * m + K, :] = jnp.where(level == code, jnp.ones((), BF16), jnp.zeros((), BF16))
    recon = dot(left[...], hot[...], NN)
    recon = recon[0:D] + recon[D : 2 * D] + recon[2 * D : 3 * D]
    out_ref[...] = vectors_ref[...] - recon


def shift(array, stage, by):
    pairs = []
    for y in range(NY):
        for x in range(NX):
            for c in range(2):
                ty, tx = ((y + by) % NY, x) if (c == 0) == (stage == 0) else (y, (x + by) % NX)
                pairs.append(((y * NX + x) * 2 + c, (ty * NX + tx) * 2 + c))
    return lax.ppermute(array, ("y", "x", "c"), pairs)


def swap(array):
    return lax.ppermute(array, "c", [(0, 1), (1, 0)])


def ring(array, stage):
    up = shift(array, stage, 1)
    down = shift(array, stage, -1)
    half = array.shape[0] // 2
    return up, down, shift(up[:half], stage, 1), shift(down[half:], stage, -1)


def along_z(array, by):
    pairs = []
    for z in range(NZ):
        for c in range(2):
            pairs.append((2 * z + c, 2 * ((z + by * (1 - 2 * c)) % NZ) + c))
    return lax.ppermute(array, ("z", "c"), pairs)


def spread(array, axes):
    return lax.all_to_all(array, axes, 0, 0, tiled=True)


def body(vectors, codes, weights, ridge):
    rows = vectors.shape[0]
    vectors = vectors.T
    codes = codes.T
    mass = weights.astype(F32).reshape(1, rows)
    info = jnp.stack([lax.axis_index(a) for a in ("y", "z", "x", "c")]).astype(jnp.int32)
    own, *messages = pl.pallas_call(
        message_kernel,
        out_shape=[jax.ShapeDtypeStruct((24, rows if d < 4 else rows // 2), F32) for d in range(5)],
        in_specs=[SMEM, VMEM, VMEM, VMEM],
        out_specs=[VMEM] * 5,
        compiler_params=params(16),
        name="message",
    )(info, codes, mass, vectors)
    messages = [along_z(message, d + 1) for d, message in enumerate(messages)]
    state = joint(info, [own], [], False)
    near, later = messages[:2], messages[2:]
    others = [swap(message) for message in near]
    state = joint(info, near, state, False)
    later, state = lax.optimization_barrier((later, state))
    others += [swap(message) for message in later]
    state = joint(info, later, state, False)
    slab = joint(info, others, state, True)
    slab = spread(slab, ("y", "x"))
    chunk = pl.pallas_call(
        sum_kernel,
        out_shape=jax.ShapeDtypeStruct((NZ, 64, 128), F32),
        in_specs=[VMEM],
        out_specs=VMEM,
        compiler_params=params(8),
        name="chunk",
    )(slab)
    line = spread(chunk, "z")
    wide = jnp.concatenate([line, *ring(line, 0)], axis=0)
    places, arrays = [], []
    for array, outer, units in zip(
        (wide, *ring(wide, 1)), (0, -1, 1, 2, 2), ((0, 1, 2, 3),) * 3 + ((0, 1), (2, 3))
    ):
        parts = [(8 * n, OFFSETS[u], outer) for n, u in enumerate(units)]
        for other in (False, True):
            places.append((other, parts))
            arrays.append(swap(array) if other else array)
    columns, total_mass = pl.pallas_call(
        functools.partial(solve_kernel, places),
        out_shape=(jax.ShapeDtypeStruct((56, 128), F32), jax.ShapeDtypeStruct((8, 128), F32)),
        in_specs=[SMEM, SMEM] + [VMEM] * len(arrays),
        out_specs=(VMEM, VMEM),
        scratch_shapes=[
            pltpu.VMEM((16, 1024, 128), F32),
            pltpu.VMEM((M, 7 * K, K), BF16),
            pltpu.VMEM((M, 7 * K, K), BF16),
            pltpu.VMEM((24, 2 * M * K), BF16),
            pltpu.VMEM((6, 8, M * K), F32),
            pltpu.VMEM((8, 128), F32),
            pltpu.VMEM((112, 128), F32),
        ],
        compiler_params=params(40),
        name="solve",
    )(info, ridge, *arrays)
    wide = jnp.stack([columns] + [shift(columns, 0, by) for by in (1, -1, 2)])
    rest = jnp.concatenate([shift(wide, 1, by) for by in (1, -1, 2)], axis=0)
    lanes = 256
    residual, table, part = pl.pallas_call(
        residual_kernel,
        grid=(rows // lanes,),
        out_shape=(
            jax.ShapeDtypeStruct((D, rows), F32),
            jax.ShapeDtypeStruct((M, D, K), F32),
            jax.ShapeDtypeStruct((1,), F32),
        ),
        in_specs=[
            SMEM,
            pl.BlockSpec((4, 56, 128), lambda i: (0, 0, 0)),
            pl.BlockSpec((12, 56, 128), lambda i: (0, 0, 0)),
            pl.BlockSpec((4, 56, 128), lambda i: (0, 0, 0)),
            pl.BlockSpec((12, 56, 128), lambda i: (0, 0, 0)),
            pl.BlockSpec((8, 128), lambda i: (0, 0)),
            pl.BlockSpec((M, lanes), lambda i: (0, i)),
            pl.BlockSpec((D, lanes), lambda i: (0, i)),
        ],
        out_specs=(
            pl.BlockSpec((D, lanes), lambda i: (0, i)),
            pl.BlockSpec((M, D, K), lambda i: (0, 0, 0)),
            SMEM,
        ),
        scratch_shapes=[
            pltpu.VMEM((3 * D, M * K), BF16),
            pltpu.VMEM((M * K, lanes), BF16),
            pltpu.VMEM((16, 112, 128), F32),
        ],
        compiler_params=params(24, dimension_semantics=("arbitrary",)),
        name="residual",
    )(info, wide, rest, swap(wide), swap(rest), total_mass, codes, vectors)
    return (table.transpose(0, 2, 1), residual.T, part[0])


def solution(mesh):
    finer = Mesh(mesh.devices.reshape(NY, NZ, NX, 2), ("y", "z", "x", "c"))
    placed = (P(DP, None), P(DP, None), P(DP), P())
    return jax.shard_map(
        body, mesh=finer, in_specs=placed, out_specs=(P(), P(DP, None), P()), check_vma=False
    )
```

```python
import functools

import jax
import jax.numpy as jnp
from jax import lax
from jax.experimental import pallas as pl
from jax.experimental.pallas import tpu as pltpu
from jax.sharding import Mesh
from jax.sharding import PartitionSpec as P

K = 256
M = 8
D = 96
ITERS = 8
NY, NZ, NX = 4, 8, 4
DP = ("y", "z", "x")
F32 = jnp.float32
BF16 = jnp.bfloat16
NT = (((1,), (1,)), ((), ()))
NN = (((1,), (0,)), ((), ()))


def dot(a, b, dims):
    return lax.dot_general(a, b, dims, preferred_element_type=F32)


def split3(a):
    hi = a.astype(BF16).astype(F32)
    rest = a - hi
    mid = rest.astype(BF16).astype(F32)
    return hi, mid, rest - mid


def params(mib, **more):
    return pltpu.CompilerParams(vmem_limit_bytes=mib << 20, **more)


VMEM = pl.BlockSpec(memory_space=pltpu.VMEM)
SMEM = pl.BlockSpec(memory_space=pltpu.SMEM)
ANY = pl.BlockSpec(memory_space=pl.ANY)


def message_kernel(info, codes_ref, mass_ref, vectors_ref, *out_refs):
    z = info[1]
    core = info[3]

    def half(a):
        n = a.shape[1] // 2
        return jnp.where(core == 0, a[:, :n], a[:, n:])

    codes = codes_ref[...].astype(F32)
    mass = mass_ref[...]
    for d, out_ref in enumerate(out_refs):
        keep = half if d == 4 else (lambda a: a)
        to = (z + d * (1 - 2 * core)) & 7
        out_ref[0:8, :] = keep(codes)
        for c in range(2):
            out_ref[8 + 8 * c : 9 + 8 * c, :] = keep(mass)
            for j in range(6):
                row = keep(vectors_ref[pl.ds(12 * to + 6 * c + j, 1), :])
                out_ref[9 + 8 * c + j : 10 + 8 * c + j, :] = row
            out_ref[15 + 8 * c : 16 + 8 * c, :] = keep(jnp.ones_like(mass))


def joint_kernel(count, first, last, info, *refs):
    messages, refs = refs[:count], refs[count:]
    if not first:
        before, refs = refs[:4], refs[4:]
    if last:
        out_ref, refs = refs[0], refs[1:]
    near, far, right, square, left, *hots = refs
    z = info[1]
    core = info[3]
    for n, ref in enumerate((near, far, right, square)):
        ref[...] = jnp.zeros_like(ref) if first else before[n][...]
    wide = hots[0].shape[2]
    level = lax.broadcasted_iota(jnp.int32, (K, wide), 0).astype(F32).astype(BF16)
    low = z & 3
    levels = lax.broadcasted_iota(jnp.int32, (128, wide), 0)
    based = (levels + 128 * core).astype(F32).astype(BF16)
    sided = (levels + 128 * (z >> 2)).astype(F32).astype(BF16)
    turn = 0
    for message in messages:
        for at in range(0, message.shape[1], wide):
            hot, turn = hots[turn % 2], turn + 1
            lanes = pl.ds(at, wide)
            for s in range(M):
                code = message[pl.ds((z + s) & 7, 1), lanes].astype(BF16)
                hot[s] = jnp.where(level == code, jnp.ones((), BF16), jnp.zeros((), BF16))
            own = message[pl.ds(pl.multiple_of(8 + 8 * core, 8), 8), lanes]
            weighted = own * own_mass(message, lanes)
            squares = weighted * own
            square[...] += sum(squares[:, 128 * i : 128 * i + 128] for i in range(wide // 128))
            hi, mid, lo = split3(weighted)
            mass = own_mass(message, lanes).astype(BF16)
            part = left.at[turn % 2]
            part[0:128] = jnp.where(based == message[pl.ds(z, 1), lanes].astype(BF16), mass, jnp.zeros((), BF16))
            part[128:160] = jnp.concatenate([hi, mid, lo, jnp.zeros_like(lo)], axis=0).astype(BF16)
            part[160:288] = jnp.where(based == message[pl.ds(low, 1), lanes].astype(BF16), mass, jnp.zeros((), BF16))
            code = message[pl.ds(low + 4, 1), lanes].astype(BF16)
            part[288:416] = jnp.where(sided == code, jnp.ones((), BF16), jnp.zeros((), BF16))
            for s in range(M):
                if 1 <= s <= 3:
                    near[s - 1] += dot(part[0:160], hot[s], NT)
                else:
                    right[s] += dot(part[128:160], hot[s], NT)
            far[...] += dot(part[160:288], part[288:416], NT)
    if last:
        for s in range(3):
            for h in range(2):
                t = 2 * s + h
                out_ref[2 * t] = near[s, 0:64, 128 * h : 128 * h + 128]
                out_ref[2 * t + 1] = near[s, 64:128, 128 * h : 128 * h + 128]
        out_ref[12] = far[0:64, :]
        out_ref[13] = far[64:128, :]
        for s in range(M):
            total = near[s - 1, 128:160] if 1 <= s <= 3 else right[s]
            total = total[0:8] + total[8:16] + total[16:24]
            for h in range(2):
                i = 2 * ((z + s) & 7) + h
                row = pl.multiple_of(8 * (i & 7), 8)
                out_ref[14 + (i >> 3), pl.ds(row, 8), :] = total[:, 128 * h : 128 * h + 128]
        for j in range(6):
            out_ref[14, 8 * j : 8 * j + 1, :] = square[1 + j : 2 + j, :]


def own_mass(message, lanes):
    return message[8:9, lanes]


def joint(info, messages, before, last):
    shapes = [(3, 160, K), (128, 128), (M, 32, K), (8, 128)]
    state = [jax.ShapeDtypeStruct(a, F32) for a in shapes]
    wide = 512
    scratch = [pltpu.VMEM((2, 416, wide), BF16), pltpu.VMEM((M, K, wide), BF16), pltpu.VMEM((M, K, wide), BF16)]
    if last:
        scratch = [pltpu.VMEM(a, F32) for a in shapes] + scratch
    count = len(messages)
    return pl.pallas_call(
        functools.partial(joint_kernel, count, not before, last),
        out_shape=jax.ShapeDtypeStruct((16, 64, 128), F32) if last else state,
        in_specs=[SMEM] + [VMEM] * (count + len(before)),
        out_specs=VMEM if last else [VMEM] * 4,
        scratch_shapes=scratch,
        compiler_params=params(16),
        cost_estimate=pl.CostEstimate(flops=5 * 10**8 * count, bytes_accessed=10**6, transcendentals=0),
        name="joint",
    )(info, *messages, *before)


def sum_kernel(in_ref, out_ref):
    total = in_ref[0]
    for i in range(1, in_ref.shape[0]):
        total = total + in_ref[i]
    for i in range(NZ):
        out_ref[i] = total


OFFSETS = (0, -1, 1, 2)


def position(info, holder, inner, outer):
    dy = inner + holder * (outer - inner)
    dx = outer + holder * (inner - outer)
    return ((info[0] + dy) & 3) * 4 + ((info[2] + dx) & 3)


def solve_kernel(places, info, ridge, *refs):
    n = len(places)
    pieces = refs[:n]
    out_ref, mass_ref = refs[n : n + 2]
    slab, high, low, wide, vec, square, result = refs[n + 2 :]
    core = info[3]
    for piece, (other, parts) in zip(pieces, places):
        holder = 1 - core if other else core
        for at, inner, outer in parts:
            row = pl.multiple_of(64 * position(info, holder, inner, outer), 64)
            for z in range(NZ):
                slab[2 * z + holder, pl.ds(row, 64), :] = piece[at + z]

    def keep(m, r, c, tile):
        hi = tile.astype(BF16)
        high[m, r : r + 128, c : c + 128] = hi
        low[m, r : r + 128, c : c + 128] = (tile - hi.astype(F32)).astype(BF16)

    def build(p, _):
        for s in range(1, 4):
            for h in range(2):
                for c in range(2):
                    tile = slab[2 * p + c, 128 * (2 * s - 2 + h) : 128 * (2 * s - 1 + h), :]
                    keep((p + s) & 7, K * (7 - s) + 128 * c, 128 * h, tile)
                    keep(p, K * (s - 1) + 128 * h, 128 * c, tile.T)
        return 0

    lax.fori_loop(0, M, build, 0)

    def build_far(p, _):
        for h in range(2):
            for c in range(2):
                tile = slab[2 * p + 8 * h + c, 768:896, :]
                keep(p + 4, 3 * K + 128 * c, 128 * h, tile)
                keep(p, 3 * K + 128 * h, 128 * c, tile.T)
        return 0

    lax.fori_loop(0, 4, build_far, 0)

    group = 4 * info[0] + info[2]
    start, remain, direction, precond, inverse, right = range(6)
    square[...] = jnp.zeros_like(square)
    for i in range(16):
        tile = slab[group, 896 + 8 * i : 904 + 8 * i, :]
        vec[remain, :, 128 * i : 128 * i + 128] = tile
        vec[right, :, 128 * i : 128 * i + 128] = tile
        if i < 6:
            square[1 + i : 2 + i, :] = tile[0:1]
    counts = vec[remain, 7:8, :]
    mass = jnp.sum(counts[:, 0:K], axis=1, keepdims=True)
    mass_ref[...] = jnp.broadcast_to(mass, mass_ref.shape)
    lam = ridge[0] * mass / K
    vec[precond] = jnp.broadcast_to(counts + lam, vec.shape[1:])
    vec[inverse] = jnp.broadcast_to(1.0 / (counts + lam), vec.shape[1:])
    vec[start] = jnp.zeros(vec.shape[1:], F32)
    scaled = vec[remain] * vec[inverse]
    vec[direction] = scaled
    first_inner = jnp.sum(vec[remain] * scaled, axis=1, keepdims=True)

    def operator(d):
        pieces = jnp.concatenate(split3(d), axis=0).astype(BF16)
        wide[:, 0 : M * K] = pieces
        wide[:, M * K :] = pieces
        image = []
        for m in range(M):
            part = wide[:, K * (m + 1) : K * (m + 8)]
            total = dot(part, high[m], NN) + dot(part, low[m], NN)
            image.append(total[0:8] + total[8:16] + total[16:24])
        return jnp.concatenate(image, axis=1) + vec[precond] * d

    def step(_, inner):
        d = vec[direction]
        image = operator(d)
        alpha = inner / jnp.sum(d * image, axis=1, keepdims=True)
        vec[start] = vec[start] + alpha * d
        r = vec[remain] - alpha * image
        vec[remain] = r
        scaled = r * vec[inverse]
        fresh = jnp.sum(r * scaled, axis=1, keepdims=True)
        vec[direction] = scaled + fresh / inner * d
        return fresh

    lax.fori_loop(0, ITERS, step, first_inner)
    for i in range(16):
        result[6 * i : 6 * i + 6, :] = vec[start, 1:7, 128 * i : 128 * i + 128]
    c = vec[start]
    fitted = c * (vec[right] + vec[remain] + lam * c)
    left = jnp.sum(square[...], axis=1, keepdims=True) - jnp.sum(fitted, axis=1, keepdims=True)
    left = jnp.sum(left[1:7], axis=0, keepdims=True)
    result[96:112, :] = jnp.broadcast_to(left, (16, 128))
    out_ref[...] = result[pl.ds(pl.multiple_of(56 * core, 8), 56), :]


def residual_kernel(
    info, wide_ref, rest_ref, wide_other, rest_other, mass_ref, codes_ref, vectors_ref,
    out_ref, table_ref, part_ref, left, hot, books_ref,
):
    step = pl.program_id(0)

    @pl.when(step == 0)
    def _():
        core = info[3]
        for holder, first, second in ((core, wide_ref, rest_ref), (1 - core, wide_other, rest_other)):
            row = pl.multiple_of(56 * holder, 8)
            for u in range(16):
                k = position(info, holder, OFFSETS[u % 4], OFFSETS[u // 4])
                books_ref[k, pl.ds(row, 56), :] = first[u] if u < 4 else second[u - 4]
        for m in range(M):
            for h in range(2):
                for k in range(16):
                    i = 2 * m + h
                    table_ref[m, 6 * k : 6 * k + 6, 128 * h : 128 * h + 128] = books_ref[k, 6 * i : 6 * i + 6, :]
        for m in range(M):
            for t, piece in enumerate(split3(table_ref[m])):
                left[D * t : D * t + D, K * m : K * m + K] = piece.astype(BF16)
        total = books_ref[0, 96:97, :]
        for k in range(1, 16):
            total = total + books_ref[k, 96:97, :]
        part_ref[0] = (total / (mass_ref[0:1, :] * D))[0, 0]

    cols = codes_ref.shape[1]
    level = lax.broadcasted_iota(jnp.int32, (K, cols), 0).astype(F32).astype(BF16)
    for m in range(M):
        code = codes_ref[m : m + 1, :].astype(F32).astype(BF16)
        hot[K * m : K * m + K, :] = jnp.where(level == code, jnp.ones((), BF16), jnp.zeros((), BF16))
    recon = dot(left[...], hot[...], NN)
    recon = recon[0:D] + recon[D : 2 * D] + recon[2 * D : 3 * D]
    out_ref[...] = vectors_ref[...] - recon


def shift(array, stage, by):
    pairs = []
    for y in range(NY):
        for x in range(NX):
            for c in range(2):
                ty, tx = ((y + by) % NY, x) if (c == 0) == (stage == 0) else (y, (x + by) % NX)
                pairs.append(((y * NX + x) * 2 + c, (ty * NX + tx) * 2 + c))
    return lax.ppermute(array, ("y", "x", "c"), pairs)


def swap(array):
    return lax.ppermute(array, "c", [(0, 1), (1, 0)])


def ring(array, stage):
    up = shift(array, stage, 1)
    down = shift(array, stage, -1)
    half = array.shape[0] // 2
    return up, down, shift(up[:half], stage, 1), shift(down[half:], stage, -1)


def along_z(array, by):
    pairs = []
    for z in range(NZ):
        for c in range(2):
            pairs.append((2 * z + c, 2 * ((z + by * (1 - 2 * c)) % NZ) + c))
    return lax.ppermute(array, ("z", "c"), pairs)


def spread(array, axes):
    return lax.all_to_all(array, axes, 0, 0, tiled=True)


def body(vectors, codes, weights, ridge):
    rows = vectors.shape[0]
    vectors = vectors.T
    codes = codes.T
    mass = weights.astype(F32).reshape(1, rows)
    info = jnp.stack([lax.axis_index(a) for a in ("y", "z", "x", "c")]).astype(jnp.int32)
    own, *messages = pl.pallas_call(
        message_kernel,
        out_shape=[jax.ShapeDtypeStruct((24, rows if d < 4 else rows // 2), F32) for d in range(5)],
        in_specs=[SMEM, VMEM, VMEM, VMEM],
        out_specs=[VMEM] * 5,
        compiler_params=params(16),
        name="message",
    )(info, codes, mass, vectors)
    messages = [along_z(message, d + 1) for d, message in enumerate(messages)]
    state = joint(info, [own], [], False)
    near, later = messages[:2], messages[2:]
    others = [swap(message) for message in near]
    state = joint(info, near, state, False)
    later, state = lax.optimization_barrier((later, state))
    others += [swap(message) for message in later]
    state = joint(info, later, state, False)
    slab = joint(info, others, state, True)
    slab = spread(slab, ("y", "x"))
    chunk = pl.pallas_call(
        sum_kernel,
        out_shape=jax.ShapeDtypeStruct((NZ, 64, 128), F32),
        in_specs=[VMEM],
        out_specs=VMEM,
        compiler_params=params(8),
        name="chunk",
    )(slab)
    line = spread(chunk, "z")
    wide = jnp.concatenate([line, *ring(line, 0)], axis=0)
    places, arrays = [], []
    for array, outer, units in zip(
        (wide, *ring(wide, 1)), (0, -1, 1, 2, 2), ((0, 1, 2, 3),) * 3 + ((0, 1), (2, 3))
    ):
        parts = [(8 * n, OFFSETS[u], outer) for n, u in enumerate(units)]
        for other in (False, True):
            places.append((other, parts))
            arrays.append(swap(array) if other else array)
    columns, total_mass = pl.pallas_call(
        functools.partial(solve_kernel, places),
        out_shape=(jax.ShapeDtypeStruct((56, 128), F32), jax.ShapeDtypeStruct((8, 128), F32)),
        in_specs=[SMEM, SMEM] + [VMEM] * len(arrays),
        out_specs=(VMEM, VMEM),
        scratch_shapes=[
            pltpu.VMEM((16, 1024, 128), F32),
            pltpu.VMEM((M, 7 * K, K), BF16),
            pltpu.VMEM((M, 7 * K, K), BF16),
            pltpu.VMEM((24, 2 * M * K), BF16),
            pltpu.VMEM((6, 8, M * K), F32),
            pltpu.VMEM((8, 128), F32),
            pltpu.VMEM((112, 128), F32),
        ],
        compiler_params=params(40),
        name="solve",
    )(info, ridge, *arrays)
    wide = jnp.stack([columns] + [shift(columns, 0, by) for by in (1, -1, 2)])
    rest = jnp.concatenate([shift(wide, 1, by) for by in (1, -1, 2)], axis=0)
    lanes = 512
    residual, table, part = pl.pallas_call(
        residual_kernel,
        grid=(rows // lanes,),
        out_shape=(
            jax.ShapeDtypeStruct((D, rows), F32),
            jax.ShapeDtypeStruct((M, D, K), F32),
            jax.ShapeDtypeStruct((1,), F32),
        ),
        in_specs=[
            SMEM,
            pl.BlockSpec((4, 56, 128), lambda i: (0, 0, 0)),
            pl.BlockSpec((12, 56, 128), lambda i: (0, 0, 0)),
            pl.BlockSpec((4, 56, 128), lambda i: (0, 0, 0)),
            pl.BlockSpec((12, 56, 128), lambda i: (0, 0, 0)),
            pl.BlockSpec((8, 128), lambda i: (0, 0)),
            pl.BlockSpec((M, lanes), lambda i: (0, i)),
            pl.BlockSpec((D, lanes), lambda i: (0, i)),
        ],
        out_specs=(
            pl.BlockSpec((D, lanes), lambda i: (0, i)),
            pl.BlockSpec((M, D, K), lambda i: (0, 0, 0)),
            SMEM,
        ),
        scratch_shapes=[
            pltpu.VMEM((3 * D, M * K), BF16),
            pltpu.VMEM((M * K, lanes), BF16),
            pltpu.VMEM((16, 112, 128), F32),
        ],
        compiler_params=params(24, dimension_semantics=("arbitrary",)),
        name="residual",
    )(info, wide, rest, swap(wide), swap(rest), total_mass, codes, vectors)
    return (table.transpose(0, 2, 1), residual.T, part[0])


def solution(mesh):
    finer = Mesh(mesh.devices.reshape(NY, NZ, NX, 2), ("y", "z", "x", "c"))
    placed = (P(DP, None), P(DP, None), P(DP), P())
    return jax.shard_map(
        body, mesh=finer, in_specs=placed, out_specs=(P(), P(DP, None), P()), check_vma=False
    )
```

```python
import functools

import jax
import jax.numpy as jnp
from jax import lax
from jax.experimental import pallas as pl
from jax.experimental.pallas import tpu as pltpu
from jax.sharding import Mesh
from jax.sharding import PartitionSpec as P

K = 256
M = 8
D = 96
ITERS = 8
NY, NZ, NX = 4, 8, 4
DP = ("y", "z", "x")
F32 = jnp.float32
BF16 = jnp.bfloat16
NT = (((1,), (1,)), ((), ()))
NN = (((1,), (0,)), ((), ()))


def dot(a, b, dims):
    return lax.dot_general(a, b, dims, preferred_element_type=F32)


def split3(a):
    hi = a.astype(BF16).astype(F32)
    rest = a - hi
    mid = rest.astype(BF16).astype(F32)
    return hi, mid, rest - mid


def params(mib, **more):
    return pltpu.CompilerParams(vmem_limit_bytes=mib << 20, **more)


VMEM = pl.BlockSpec(memory_space=pltpu.VMEM)
SMEM = pl.BlockSpec(memory_space=pltpu.SMEM)
ANY = pl.BlockSpec(memory_space=pl.ANY)


def message_kernel(info, codes_ref, mass_ref, vectors_ref, *out_refs):
    z = info[1]
    core = info[3]

    def half(a):
        n = a.shape[1] // 2
        return jnp.where(core == 0, a[:, :n], a[:, n:])

    codes = codes_ref[...].astype(F32)
    mass = mass_ref[...]
    for d, out_ref in enumerate(out_refs):
        keep = half if d == 4 else (lambda a: a)
        to = (z + d * (1 - 2 * core)) & 7
        out_ref[0:8, :] = keep(codes)
        for c in range(2):
            out_ref[8 + 8 * c : 9 + 8 * c, :] = keep(mass)
            for j in range(6):
                row = keep(vectors_ref[pl.ds(12 * to + 6 * c + j, 1), :])
                out_ref[9 + 8 * c + j : 10 + 8 * c + j, :] = row
            out_ref[15 + 8 * c : 16 + 8 * c, :] = keep(jnp.ones_like(mass))


def joint_kernel(count, first, last, info, *refs):
    messages, refs = refs[:count], refs[count:]
    if not first:
        before, refs = refs[:4], refs[4:]
    if last:
        out_ref, refs = refs[0], refs[1:]
    near, far, right, square, left, *hots = refs
    z = info[1]
    core = info[3]
    for n, ref in enumerate((near, far, right, square)):
        ref[...] = jnp.zeros_like(ref) if first else before[n][...]
    wide = hots[0].shape[2]
    level = lax.broadcasted_iota(jnp.int32, (K, wide), 0).astype(F32).astype(BF16)
    low = z & 3
    levels = lax.broadcasted_iota(jnp.int32, (128, wide), 0)
    based = (levels + 128 * core).astype(F32).astype(BF16)
    sided = (levels + 128 * (z >> 2)).astype(F32).astype(BF16)
    turn = 0
    for message in messages:
        for at in range(0, message.shape[1], wide):
            hot, turn = hots[turn % 2], turn + 1
            lanes = pl.ds(at, wide)
            for s in range(M):
                code = message[pl.ds((z + s) & 7, 1), lanes].astype(BF16)
                hot[s] = jnp.where(level == code, jnp.ones((), BF16), jnp.zeros((), BF16))
            own = message[pl.ds(pl.multiple_of(8 + 8 * core, 8), 8), lanes]
            weighted = own * own_mass(message, lanes)
            squares = weighted * own
            square[...] += sum(squares[:, 128 * i : 128 * i + 128] for i in range(wide // 128))
            hi, mid, lo = split3(weighted)
            mass = own_mass(message, lanes).astype(BF16)
            part = left.at[turn % 2]
            part[0:128] = jnp.where(based == message[pl.ds(z, 1), lanes].astype(BF16), mass, jnp.zeros((), BF16))
            part[128:160] = jnp.concatenate([hi, mid, lo, jnp.zeros_like(lo)], axis=0).astype(BF16)
            part[160:288] = jnp.where(based == message[pl.ds(low, 1), lanes].astype(BF16), mass, jnp.zeros((), BF16))
            code = message[pl.ds(low + 4, 1), lanes].astype(BF16)
            part[288:416] = jnp.where(sided == code, jnp.ones((), BF16), jnp.zeros((), BF16))
            for s in range(M):
                if 1 <= s <= 3:
                    near[s - 1] += dot(part[0:160], hot[s], NT)
                else:
                    right[s] += dot(part[128:160], hot[s], NT)
            far[...] += dot(part[160:288], part[288:416], NT)
    if last:
        for s in range(3):
            for h in range(2):
                t = 2 * s + h
                out_ref[2 * t] = near[s, 0:64, 128 * h : 128 * h + 128]
                out_ref[2 * t + 1] = near[s, 64:128, 128 * h : 128 * h + 128]
        out_ref[12] = far[0:64, :]
        out_ref[13] = far[64:128, :]
        for s in range(M):
            total = near[s - 1, 128:160] if 1 <= s <= 3 else right[s]
            total = total[0:8] + total[8:16] + total[16:24]
            for h in range(2):
                i = 2 * ((z + s) & 7) + h
                row = pl.multiple_of(8 * (i & 7), 8)
                out_ref[14 + (i >> 3), pl.ds(row, 8), :] = total[:, 128 * h : 128 * h + 128]
        for j in range(6):
            out_ref[14, 8 * j : 8 * j + 1, :] = square[1 + j : 2 + j, :]


def own_mass(message, lanes):
    return message[8:9, lanes]


def joint(info, messages, before, last):
    shapes = [(3, 160, K), (128, 128), (M, 32, K), (8, 128)]
    state = [jax.ShapeDtypeStruct(a, F32) for a in shapes]
    wide = 512
    scratch = [pltpu.VMEM((2, 416, wide), BF16), pltpu.VMEM((M, K, wide), BF16), pltpu.VMEM((M, K, wide), BF16)]
    if last:
        scratch = [pltpu.VMEM(a, F32) for a in shapes] + scratch
    count = len(messages)
    return pl.pallas_call(
        functools.partial(joint_kernel, count, not before, last),
        out_shape=jax.ShapeDtypeStruct((16, 64, 128), F32) if last else state,
        in_specs=[SMEM] + [VMEM] * (count + len(before)),
        out_specs=VMEM if last else [VMEM] * 4,
        scratch_shapes=scratch,
        compiler_params=params(16),
        cost_estimate=pl.CostEstimate(flops=5 * 10**8 * count, bytes_accessed=10**6, transcendentals=0),
        name="joint",
    )(info, *messages, *before)


def sum_kernel(in_ref, out_ref):
    total = in_ref[0]
    for i in range(1, in_ref.shape[0]):
        total = total + in_ref[i]
    for i in range(NZ):
        out_ref[i] = total


OFFSETS = (0, -1, 1, 2)


def position(info, holder, inner, outer):
    dy = inner + holder * (outer - inner)
    dx = outer + holder * (inner - outer)
    return ((info[0] + dy) & 3) * 4 + ((info[2] + dx) & 3)


def solve_kernel(places, info, ridge, *refs):
    n = len(places)
    pieces = refs[:n]
    out_ref, mass_ref = refs[n : n + 2]
    slab, high, low, wide, vec, square, result = refs[n + 2 :]
    core = info[3]
    for piece, (other, parts) in zip(pieces, places):
        holder = 1 - core if other else core
        for at, inner, outer in parts:
            row = pl.multiple_of(64 * position(info, holder, inner, outer), 64)
            for z in range(NZ):
                slab[2 * z + holder, pl.ds(row, 64), :] = piece[at + z]

    def keep(m, r, c, tile):
        hi = tile.astype(BF16)
        high[m, r : r + 128, c : c + 128] = hi
        low[m, r : r + 128, c : c + 128] = (tile - hi.astype(F32)).astype(BF16)

    def build(p, _):
        for s in range(1, 4):
            for h in range(2):
                for c in range(2):
                    tile = slab[2 * p + c, 128 * (2 * s - 2 + h) : 128 * (2 * s - 1 + h), :]
                    keep((p + s) & 7, K * (7 - s) + 128 * c, 128 * h, tile)
                    keep(p, K * (s - 1) + 128 * h, 128 * c, tile.T)
        return 0

    lax.fori_loop(0, M, build, 0)

    def build_far(p, _):
        for h in range(2):
            for c in range(2):
                tile = slab[2 * p + 8 * h + c, 768:896, :]
                keep(p + 4, 3 * K + 128 * c, 128 * h, tile)
                keep(p, 3 * K + 128 * h, 128 * c, tile.T)
        return 0

    lax.fori_loop(0, 4, build_far, 0)

    group = 4 * info[0] + info[2]
    start, remain, direction, precond, inverse, right = range(6)
    square[...] = jnp.zeros_like(square)
    for i in range(16):
        tile = slab[group, 896 + 8 * i : 904 + 8 * i, :]
        vec[remain, :, 128 * i : 128 * i + 128] = tile
        vec[right, :, 128 * i : 128 * i + 128] = tile
        if i < 6:
            square[1 + i : 2 + i, :] = tile[0:1]
    counts = vec[remain, 7:8, :]
    mass = jnp.sum(counts[:, 0:K], axis=1, keepdims=True)
    mass_ref[...] = jnp.broadcast_to(mass, mass_ref.shape)
    lam = ridge[0] * mass / K
    vec[precond] = jnp.broadcast_to(counts + lam, vec.shape[1:])
    vec[inverse] = jnp.broadcast_to(1.0 / (counts + lam), vec.shape[1:])
    vec[start] = jnp.zeros(vec.shape[1:], F32)
    scaled = vec[remain] * vec[inverse]
    vec[direction] = scaled
    first_inner = jnp.sum(vec[remain] * scaled, axis=1, keepdims=True)

    def operator(d):
        pieces = jnp.concatenate(split3(d), axis=0).astype(BF16)
        wide[:, 0 : M * K] = pieces
        wide[:, M * K :] = pieces
        image = []
        for m in range(M):
            part = wide[:, K * (m + 1) : K * (m + 8)]
            total = dot(part, high[m], NN) + dot(part, low[m], NN)
            image.append(total[0:8] + total[8:16] + total[16:24])
        return jnp.concatenate(image, axis=1) + vec[precond] * d

    def step(_, inner):
        d = vec[direction]
        image = operator(d)
        alpha = inner / jnp.sum(d * image, axis=1, keepdims=True)
        vec[start] = vec[start] + alpha * d
        r = vec[remain] - alpha * image
        vec[remain] = r
        scaled = r * vec[inverse]
        fresh = jnp.sum(r * scaled, axis=1, keepdims=True)
        vec[direction] = scaled + fresh / inner * d
        return fresh

    lax.fori_loop(0, ITERS, step, first_inner)
    for i in range(16):
        result[6 * i : 6 * i + 6, :] = vec[start, 1:7, 128 * i : 128 * i + 128]
    c = vec[start]
    fitted = c * (vec[right] + vec[remain] + lam * c)
    left = jnp.sum(square[...], axis=1, keepdims=True) - jnp.sum(fitted, axis=1, keepdims=True)
    left = jnp.sum(left[1:7], axis=0, keepdims=True)
    result[96:112, :] = jnp.broadcast_to(left, (16, 128))
    out_ref[...] = result[pl.ds(pl.multiple_of(56 * core, 8), 56), :]


def residual_kernel(
    info, wide_ref, rest_ref, wide_other, rest_other, mass_ref, codes_ref, vectors_ref,
    out_ref, table_ref, part_ref, left, hot, books_ref,
):
    step = pl.program_id(0)

    @pl.when(step == 0)
    def _():
        core = info[3]
        for holder, first, second in ((core, wide_ref, rest_ref), (1 - core, wide_other, rest_other)):
            row = pl.multiple_of(56 * holder, 8)
            for u in range(16):
                k = position(info, holder, OFFSETS[u % 4], OFFSETS[u // 4])
                books_ref[k, pl.ds(row, 56), :] = first[u] if u < 4 else second[u - 4]
        for m in range(M):
            for h in range(2):
                for k in range(16):
                    i = 2 * m + h
                    table_ref[m, 6 * k : 6 * k + 6, 128 * h : 128 * h + 128] = books_ref[k, 6 * i : 6 * i + 6, :]
        for m in range(M):
            for t, piece in enumerate(split3(table_ref[m])):
                left[D * t : D * t + D, K * m : K * m + K] = piece.astype(BF16)
        total = books_ref[0, 96:97, :]
        for k in range(1, 16):
            total = total + books_ref[k, 96:97, :]
        part_ref[0] = (total / (mass_ref[0:1, :] * D))[0, 0]

    cols = codes_ref.shape[1]
    level = lax.broadcasted_iota(jnp.int32, (K, cols), 0).astype(F32).astype(BF16)
    for m in range(M):
        code = codes_ref[m : m + 1, :].astype(F32).astype(BF16)
        hot[K * m : K * m + K, :] = jnp.where(level == code, jnp.ones((), BF16), jnp.zeros((), BF16))
    recon = dot(left[...], hot[...], NN)
    recon = recon[0:D] + recon[D : 2 * D] + recon[2 * D : 3 * D]
    out_ref[...] = vectors_ref[...] - recon


def shift(array, stage, by):
    pairs = []
    for y in range(NY):
        for x in range(NX):
            for c in range(2):
                ty, tx = ((y + by) % NY, x) if (c == 0) == (stage == 0) else (y, (x + by) % NX)
                pairs.append(((y * NX + x) * 2 + c, (ty * NX + tx) * 2 + c))
    return lax.ppermute(array, ("y", "x", "c"), pairs)


def swap(array):
    return lax.ppermute(array, "c", [(0, 1), (1, 0)])


def ring(array, stage):
    up = shift(array, stage, 1)
    down = shift(array, stage, -1)
    half = array.shape[0] // 2
    return up, down, shift(up[:half], stage, 1), shift(down[half:], stage, -1)


def along_z(array, by):
    pairs = []
    for z in range(NZ):
        for c in range(2):
            pairs.append((2 * z + c, 2 * ((z + by * (1 - 2 * c)) % NZ) + c))
    return lax.ppermute(array, ("z", "c"), pairs)


def spread(array, axes):
    return lax.all_to_all(array, axes, 0, 0, tiled=True)


def body(vectors, codes, weights, ridge):
    rows = vectors.shape[0]
    vectors = vectors.T
    codes = codes.T
    mass = weights.astype(F32).reshape(1, rows)
    info = jnp.stack([lax.axis_index(a) for a in ("y", "z", "x", "c")]).astype(jnp.int32)
    own, *messages = pl.pallas_call(
        message_kernel,
        out_shape=[jax.ShapeDtypeStruct((24, rows if d < 4 else rows // 2), F32) for d in range(5)],
        in_specs=[SMEM, VMEM, VMEM, VMEM],
        out_specs=[VMEM] * 5,
        compiler_params=params(16),
        name="message",
    )(info, codes, mass, vectors)
    messages = [along_z(message, d + 1) for d, message in enumerate(messages)]
    state = joint(info, [own], [], False)
    near, later = messages[:2], messages[2:]
    others = [swap(message) for message in near]
    state = joint(info, near, state, False)
    state = joint(info, others, state, False)
    later, state = lax.optimization_barrier((later, state))
    others = [swap(message) for message in later]
    state = joint(info, later, state, False)
    slab = joint(info, others, state, True)
    slab = spread(slab, ("y", "x"))
    chunk = pl.pallas_call(
        sum_kernel,
        out_shape=jax.ShapeDtypeStruct((NZ, 64, 128), F32),
        in_specs=[VMEM],
        out_specs=VMEM,
        compiler_params=params(8),
        name="chunk",
    )(slab)
    line = spread(chunk, "z")
    wide = jnp.concatenate([line, *ring(line, 0)], axis=0)
    places, arrays = [], []
    for array, outer, units in zip(
        (wide, *ring(wide, 1)), (0, -1, 1, 2, 2), ((0, 1, 2, 3),) * 3 + ((0, 1), (2, 3))
    ):
        parts = [(8 * n, OFFSETS[u], outer) for n, u in enumerate(units)]
        for other in (False, True):
            places.append((other, parts))
            arrays.append(swap(array) if other else array)
    columns, total_mass = pl.pallas_call(
        functools.partial(solve_kernel, places),
        out_shape=(jax.ShapeDtypeStruct((56, 128), F32), jax.ShapeDtypeStruct((8, 128), F32)),
        in_specs=[SMEM, SMEM] + [VMEM] * len(arrays),
        out_specs=(VMEM, VMEM),
        scratch_shapes=[
            pltpu.VMEM((16, 1024, 128), F32),
            pltpu.VMEM((M, 7 * K, K), BF16),
            pltpu.VMEM((M, 7 * K, K), BF16),
            pltpu.VMEM((24, 2 * M * K), BF16),
            pltpu.VMEM((6, 8, M * K), F32),
            pltpu.VMEM((8, 128), F32),
            pltpu.VMEM((112, 128), F32),
        ],
        compiler_params=params(40),
        name="solve",
    )(info, ridge, *arrays)
    wide = jnp.stack([columns] + [shift(columns, 0, by) for by in (1, -1, 2)])
    rest = jnp.concatenate([shift(wide, 1, by) for by in (1, -1, 2)], axis=0)
    lanes = 512
    residual, table, part = pl.pallas_call(
        residual_kernel,
        grid=(rows // lanes,),
        out_shape=(
            jax.ShapeDtypeStruct((D, rows), F32),
            jax.ShapeDtypeStruct((M, D, K), F32),
            jax.ShapeDtypeStruct((1,), F32),
        ),
        in_specs=[
            SMEM,
            pl.BlockSpec((4, 56, 128), lambda i: (0, 0, 0)),
            pl.BlockSpec((12, 56, 128), lambda i: (0, 0, 0)),
            pl.BlockSpec((4, 56, 128), lambda i: (0, 0, 0)),
            pl.BlockSpec((12, 56, 128), lambda i: (0, 0, 0)),
            pl.BlockSpec((8, 128), lambda i: (0, 0)),
            pl.BlockSpec((M, lanes), lambda i: (0, i)),
            pl.BlockSpec((D, lanes), lambda i: (0, i)),
        ],
        out_specs=(
            pl.BlockSpec((D, lanes), lambda i: (0, i)),
            pl.BlockSpec((M, D, K), lambda i: (0, 0, 0)),
            SMEM,
        ),
        scratch_shapes=[
            pltpu.VMEM((3 * D, M * K), BF16),
            pltpu.VMEM((M * K, lanes), BF16),
            pltpu.VMEM((16, 112, 128), F32),
        ],
        compiler_params=params(24, dimension_semantics=("arbitrary",)),
        name="residual",
    )(info, wide, rest, swap(wide), swap(rest), total_mass, codes, vectors)
    return (table.transpose(0, 2, 1), residual.T, part[0])


def solution(mesh):
    finer = Mesh(mesh.devices.reshape(NY, NZ, NX, 2), ("y", "z", "x", "c"))
    placed = (P(DP, None), P(DP, None), P(DP), P())
    return jax.shard_map(
        body, mesh=finer, in_specs=placed, out_specs=(P(), P(DP, None), P()), check_vma=False
    )
```
